128 devices in a mesh: dp: 16 (over z_hi, y, core), ctx: 8 (over x, z_lo).
Axes of the slice: x: 4, y: 4, z: 4 (z_hi: 2, z_lo: 2; z = z_hi * 2 + z_lo), core: 2. Of those that a mesh axis runs over, the one named last changes fastest.
Arguments:
- hidden: bfloat16 [16, 3072, 8192], P('dp', 'ctx'), may hold values from -6 to 6
- queries: bfloat16 [16, 3072, 4096], P('dp', 'ctx'), may hold values from -136 to 136
- weights_old: float32 [8192, 1024], P(('dp', 'ctx')), may hold values from -0.0625 to 0.0625
- gradient_old: float32 [8192, 1024], P(('dp', 'ctx')), may hold values from -6 to 6
- first_old: float32 [8192, 1024], P(('dp', 'ctx')), may hold values from -4 to 4
- second_old: float32 [8192, 1024], P(('dp', 'ctx')), may hold values from 0.25 to 4
- old_owner: int32 [128], replicated, may hold values from 0 to 127, each once
- new_owner: int32 [128], replicated, may hold values from 0 to 127, each once
- offsets: int32 [16, 8, 2], P('dp'), may hold values from 0 to 2880, as said below
Outputs:
- weights_new: float32 [1024, 8192], P(('dp', 'ctx'))
- first_new: float32 [1024, 8192], P(('dp', 'ctx'))
- second_new: float32 [1024, 8192], P(('dp', 'ctx'))
- attended: bfloat16 [16, 3072, 4096], P('dp', 'ctx')
The draws below stay inside these ranges and needn't reach their ends.
Inputs may be any that keep to these rules, and one draw needn't show every extreme that they name: `offsets`: for sequence b and ctx index c the two entries are p * 192 and (15 - p) * 192, where p runs over a permutation of the ctx indices drawn for each sequence. `old_owner`: each block index appears once. `new_owner`: each block index appears once.
All inputs are finite; a program needn't handle non-finite values.
Results may differ from the reference program's by a relative error of at most 0.0055.
The reference program's roundings to bfloat16 on the way count: a program that leaves them out, or rounds other values in their place, can miss the bound.
Values may be sent and summed in bfloat16 or wider, within the bound.
No kernel may reach another device: no remote copies, remote signals or barrier semaphores. Data moves between devices by JAX's collectives and lax.ppermute only.
A program may use at most 320 MiB of HBM per device.

```python
import math
import jax
import jax.numpy as jnp
from jax import lax

D = 8192
HEAD = 128
KV_HEADS = 4
Q_HEADS = 32
TOK = 384
HALF = 192
SEQ = 3072
BATCH = 16
PROJ = 1024
ROW_BLOCK = 64
COL_BLOCK = 8


def draw_queries(key, part):
    shape = (BATCH, SEQ, Q_HEADS * HEAD)
    normal_part = jax.random.normal(key, shape, jnp.float32)
    return jnp.clip(normal_part, -6.0, 6.0).astype(jnp.bfloat16)


def draw_offsets(key, part):
    ctx_count = SEQ // TOK
    half_tok = TOK // 2
    subkeys = jax.random.split(key, BATCH)

    def order_of(subkey):
        return jax.random.permutation(subkey, ctx_count)
    orders = jax.vmap(order_of)(subkeys).astype(jnp.int32)
    first_start = orders * half_tok
    second_start = (2 * ctx_count - 1 - orders) * half_tok
    return jnp.stack([first_start, second_start], axis=-1).astype(jnp.int32)


def levels(key, dims, cuts, smallest, high):
    factor_of, own = 1.0, jax.random.fold_in(key, 6)
    for dim, shards_of in cuts:
        heights = jnp.exp(jax.random.uniform(jax.random.fold_in(own, dim), (shards_of,), jnp.float32, smallest / len(cuts), high / len(cuts)))
        factor_of = factor_of * jnp.repeat(heights, dims[dim] // shards_of).reshape([-1 if axis == dim else 1 for axis in range(len(dims))])
    return factor_of


def gaussian(key, dims, width, limit, cuts=(), kind=jnp.bfloat16):
    result = width * jax.random.normal(key, dims, jnp.float32)
    if cuts:
        result = result * levels(key, dims, cuts, -0.22, 0.18)
    return jnp.clip(result, -limit, limit).astype(kind)


def setup_inputs(seed: int = 0) -> dict:
    splits = jax.random.split(jax.random.key(seed), 10)
    hidden = gaussian(splits[0], (BATCH, SEQ, D), 1.0, 6.0, ((0, 16), (1, 8)))
    queries = draw_queries(jax.random.fold_in(splits[9], 71), 0)
    weights_old = gaussian(splits[2], (D, PROJ), D ** -0.5, 0.0625, ((0, 128),), jnp.float32)
    gradient_old = gaussian(splits[3], (D, PROJ), 1.0, 6.0, ((0, 128),), jnp.float32)
    first_old = gaussian(splits[4], (D, PROJ), 0.3, 4.0, ((0, 128),), jnp.float32)
    second_old = jnp.clip(jnp.exp(math.log(4.0) - 2.7725887 * jax.random.uniform(splits[5], (D, PROJ), jnp.float32) ** levels(splits[5], (D, PROJ), ((0, 128),), -0.2, 0.2)), 0.25, 4.0)
    old_owner = jax.random.permutation(splits[6], D // ROW_BLOCK).astype(jnp.int32)
    new_owner = jax.random.permutation(splits[7], D // ROW_BLOCK).astype(jnp.int32)
    offsets = draw_offsets(jax.random.fold_in(splits[9], 71), 0)
    return dict(hidden=hidden, queries=queries, weights_old=weights_old, gradient_old=gradient_old, first_old=first_old, second_old=second_old, old_owner=old_owner, new_owner=new_owner, offsets=offsets)


learn_rate = 0.0003
beta_one = 0.9
beta_two = 0.95
adam_eps = 1e-08
decay_rate = 0.1
step_number = 1000
corr_one = 1.0 - beta_one ** step_number
corr_two = 1.0 - beta_two ** step_number
rope_base = 500000.0

def adam_step(weights, gradient, first_mom, second_mom):
    first_next = beta_one * first_mom + (1.0 - beta_one) * gradient
    second_next = beta_two * second_mom + (1.0 - beta_two) * gradient * gradient
    direction = first_next / corr_one / (jnp.sqrt(second_next / corr_two) + adam_eps)
    weights_next = weights - learn_rate * (direction + decay_rate * weights)
    return (weights_next, first_next, second_next)

def rotate_keys(key_heads, positions):
    head_dim = key_heads.shape[-1]
    half_dim = head_dim // 2
    exponent = jnp.arange(half_dim, dtype=jnp.float32) * (2.0 / head_dim)
    inv_freq = jnp.power(rope_base, -exponent)
    angles = positions.astype(jnp.float32)[..., None] * inv_freq
    cosine = jnp.cos(angles)[..., None, :]
    sine_part = jnp.sin(angles)[..., None, :]
    first_half = key_heads[..., :half_dim]
    second_half = key_heads[..., half_dim:]
    return jnp.concatenate([first_half * cosine - second_half * sine_part, second_half * cosine + first_half * sine_part], axis=-1)

def reference(hidden, queries, weights_old, gradient_old, first_old, second_old, old_owner, new_owner, offsets):
    devices = D // ROW_BLOCK

    def to_logical(stored):
        blocks = stored.reshape(devices, ROW_BLOCK, PROJ)
        return jnp.zeros_like(blocks).at[old_owner].set(blocks).reshape(D, PROJ)

    def to_new(logical):
        return jnp.take(logical.T.reshape(devices, COL_BLOCK, D), new_owner, axis=0).reshape(PROJ, D)
    weights_next, first_next, second_next = adam_step(to_logical(weights_old), to_logical(gradient_old), to_logical(first_old), to_logical(second_old))
    copies = weights_next.astype(jnp.bfloat16)
    row_ids = jnp.arange(SEQ, dtype=jnp.int32)
    local_row = row_ids % TOK
    positions = offsets[:, row_ids // TOK, local_row // HALF] + local_row % HALF
    key_width = KV_HEADS * HEAD
    groups = Q_HEADS // KV_HEADS

    def one_sequence(packed):
        tokens, query_rows, token_pos = packed
        projected = jnp.dot(tokens, copies, preferred_element_type=jnp.float32)
        key_heads = rotate_keys(projected[:, :key_width].reshape(SEQ, KV_HEADS, HEAD), token_pos)
        key_round = lax.optimization_barrier(key_heads.astype(jnp.bfloat16)).astype(jnp.float32)
        value_round = lax.optimization_barrier(projected[:, key_width:].astype(jnp.bfloat16)).astype(jnp.float32).reshape(SEQ, KV_HEADS, HEAD)
        query_heads = query_rows.astype(jnp.float32).reshape(SEQ, KV_HEADS, groups, HEAD)
        visible = token_pos[None, :] <= token_pos[:, None]

        def one_head(inputs):
            query_group, key_head, value_head = inputs
            scores = jnp.einsum('tgd,nd->gtn', query_group, key_head) / math.sqrt(HEAD)
            masked = jnp.where(visible[None], scores, -jnp.inf)
            best_score = lax.optimization_barrier(jnp.max(masked, axis=2, keepdims=True))
            weights = jnp.where(visible[None], jnp.exp(masked - best_score), 0.0)
            rounded = lax.optimization_barrier(weights.astype(jnp.bfloat16)).astype(jnp.float32)
            numerator = jnp.einsum('gtn,nd->tgd', rounded, value_head)
            return numerator / lax.optimization_barrier(jnp.sum(weights, axis=2)).T[:, :, None]
        heads_out = lax.map(one_head, (query_heads.transpose(1, 0, 2, 3), key_round.transpose(1, 0, 2), value_round.transpose(1, 0, 2)))
        return heads_out.transpose(1, 0, 2, 3).reshape(SEQ, Q_HEADS * HEAD).astype(jnp.bfloat16)
    attended = lax.map(one_sequence, (hidden, queries, positions))
    return (to_new(weights_next), to_new(first_next), to_new(second_next), attended)
```

```python
import math

import jax
import jax.numpy as jnp
from jax import lax
from jax.experimental import pallas as pl
from jax.experimental.pallas import tpu as pltpu
from jax.sharding import Mesh
from jax.sharding import PartitionSpec as P

HEAD = 128
KV_HEADS = 4
Q_HEADS = 32
GROUPS = Q_HEADS // KV_HEADS
DP = ("zh", "y", "c")
CTX = ("x", "zl")
ALL = DP + CTX
TORUS = ("zh", "zl", "x", "y", "c")
HOLE = 1 << 20
LOW = -1e30


learn_rate = 0.0003
beta_one = 0.9
beta_two = 0.95
adam_eps = 1e-08
decay_rate = 0.1
step_number = 1000
corr_one = 1.0 - beta_one**step_number
corr_two = 1.0 - beta_two**step_number
rope_base = 500000.0


def in_blocks(value, dim, peers):
    before, after = (value.shape[:dim], value.shape[dim + 1 :])
    return jnp.moveaxis(value.reshape(*before, peers, -1, *after), dim, 0)


def adam_step(weights, gradient, first_mom, second_mom):
    first_next = beta_one * first_mom + (1.0 - beta_one) * gradient
    second_next = beta_two * second_mom + (1.0 - beta_two) * gradient * gradient
    direction = first_next / corr_one / (jnp.sqrt(second_next / corr_two) + adam_eps)
    weights_next = weights - learn_rate * (direction + decay_rate * weights)
    return (weights_next, first_next, second_next)


def invert(owners):
    devices = owners.shape[0]
    return jnp.zeros((devices,), jnp.int32).at[owners].set(jnp.arange(devices, dtype=jnp.int32))


def relocate(stacked, new_owner, old_owner):
    states_count, row_count, proj_width = stacked.shape
    devices = new_owner.shape[0]
    col_count = proj_width // devices
    outgoing = stacked.reshape(states_count, row_count, devices, col_count).transpose(2, 0, 3, 1)
    outgoing = jnp.take(outgoing, new_owner, axis=0)
    incoming = lax.all_to_all(outgoing, ALL, split_axis=0, concat_axis=0, tiled=True)
    ordered = jnp.take(incoming, invert(old_owner), axis=0)
    return ordered.transpose(1, 2, 0, 3).reshape(states_count, col_count, devices * row_count)


def project_kernel(source, hidden, gathered, cosine, sine, out, rows, cols, sums, row_sem, col_sem):
    blocks, block_rows, _ = gathered.shape
    tokens, width = hidden.shape
    chunks = row_sem.shape[0]
    per = blocks // chunks
    span = width // chunks

    def row_copy(block, chunk):
        return pltpu.make_async_copy(
            gathered.at[source[block]],
            rows.at[pl.ds(pl.multiple_of(block * block_rows, block_rows), block_rows)],
            row_sem.at[chunk],
        )

    def col_copy(chunk):
        return pltpu.make_async_copy(
            hidden.at[:, pl.ds(chunk * span, span)],
            cols.at[:, pl.ds(chunk * span, span)],
            col_sem.at[chunk],
        )

    for chunk in range(chunks):
        col_copy(chunk).start()

        def issue(i, carry, chunk=chunk):
            row_copy(chunk * per + i, chunk).start()
            return carry

        lax.fori_loop(0, per, issue, 0)
    for chunk in range(chunks):
        col_copy(chunk).wait()
        whole = rows.at[pl.ds(chunk * span, span)]
        pltpu.make_async_copy(whole, whole, row_sem.at[chunk]).wait()
        part = jnp.dot(
            cols[:, chunk * span : (chunk + 1) * span],
            rows[chunk * span : (chunk + 1) * span, :],
            preferred_element_type=jnp.float32,
        )
        if chunk == 0:
            sums[...] = part
        else:
            sums[...] += part
    for head in range(KV_HEADS):
        key = sums[:, head * HEAD : (head + 1) * HEAD]
        turned = pltpu.roll(key, HEAD // 2, 1)
        out[:, head * HEAD : (head + 1) * HEAD] = (
            key * cosine[...] + turned * sine[...]
        ).astype(out.dtype)
    key_width = KV_HEADS * HEAD
    out[:, key_width:] = sums[:, key_width:].astype(out.dtype)


def project(hidden, gathered, source, cosine, sine):
    tokens, width = hidden.shape
    blocks, block_rows, features = gathered.shape
    chunks = 8
    return pl.pallas_call(
        project_kernel,
        out_shape=jax.ShapeDtypeStruct((tokens, features), jnp.bfloat16),
        grid_spec=pltpu.PrefetchScalarGridSpec(
            num_scalar_prefetch=1,
            grid=(1,),
            in_specs=[
                pl.BlockSpec(memory_space=pl.ANY),
                pl.BlockSpec(memory_space=pl.ANY),
                pl.BlockSpec((tokens, HEAD), lambda i, s: (0, 0)),
                pl.BlockSpec((tokens, HEAD), lambda i, s: (0, 0)),
            ],
            out_specs=pl.BlockSpec((tokens, features), lambda i, s: (0, 0)),
            scratch_shapes=[
                pltpu.VMEM((width, features), jnp.bfloat16),
                pltpu.VMEM((tokens, width), jnp.bfloat16),
                pltpu.VMEM((tokens, features), jnp.float32),
                pltpu.SemaphoreType.DMA((chunks,)),
                pltpu.SemaphoreType.DMA((chunks,)),
            ],
        ),
        compiler_params=pltpu.CompilerParams(vmem_limit_bytes=44 << 20),
        name="project",
    )(source, hidden, gathered, cosine, sine)


def plan(mine, bases, pairs):
    count = bases.shape[0]
    low, high = bases[:, 0], bases[:, 1]
    own = low == mine[0]
    slots = jnp.arange(count, dtype=jnp.int32)
    has_own = jnp.any(own).astype(jnp.int32)

    def listed(chosen, segment, base):
        other = chosen & ~own
        earlier = jnp.sum(
            jnp.where((slots[None, :] < slots[:, None]) & other[None, :], 1, 0), axis=1
        )
        rank = jnp.where(own, 0, has_own + earlier)
        hit = chosen[None, :] & (rank[None, :] == jnp.arange(2 * pairs, dtype=jnp.int32)[:, None])
        found = jnp.any(hit, axis=1)
        keys = jnp.sum(jnp.where(hit, segment[None, :], 0), axis=1)
        starts = jnp.where(found, jnp.sum(jnp.where(hit, base[None, :], 0), axis=1), HOLE)
        return keys, starts, jnp.sum(jnp.where(chosen, 1, 0))

    low_keys, low_starts, low_count = listed(low <= mine[0], 2 * slots, low)
    high_keys, high_starts, high_count = listed(low >= mine[0], 2 * slots + 1, high)
    low_blocks = (low_count + 1) // 2
    high_blocks = (high_count + 1) // 2
    step = jnp.arange(pairs, dtype=jnp.int32)
    is_high = (step >= low_blocks).astype(jnp.int32)
    at = step - is_high * low_blocks
    take = jnp.arange(2 * pairs, dtype=jnp.int32)

    def pick(low_list, high_list, offset):
        one = take[None, :] == (2 * at + offset)[:, None]
        chosen = jnp.where(is_high[:, None] == 1, high_list[None, :], low_list[None, :])
        return jnp.sum(jnp.where(one, chosen, 0), axis=1)

    key_a, key_b = pick(low_keys, high_keys, 0), pick(low_keys, high_keys, 1)
    base_a, base_b = pick(low_starts, high_starts, 0), pick(low_starts, high_starts, 1)
    query_base = jnp.where(is_high == 1, mine[1], mine[0])
    masked = ((base_b == HOLE) | ((at == 0) & (has_own == 1))).astype(jnp.int32)
    live = (step < low_blocks + high_blocks).astype(jnp.int32)
    return jnp.stack(
        [is_high, key_a, key_b, masked, query_base, base_a, base_b, live], axis=1
    ).reshape(-1)


def attend_kernel(count, pairs, steps, queries, keys, values, out, packed, key_rows, value_rows, best, sums):
    half = queries.shape[0] // 2
    stack = GROUPS * half
    scale = math.log2(math.e) / math.sqrt(HEAD)

    @pl.when(pl.program_id(0) == 0)
    def _():
        value_rows[:, :, HEAD:] = jnp.ones((2 * count, half, HEAD), value_rows.dtype)

    for slot in range(count):
        key_rows[2 * slot] = keys[slot, :half]
        key_rows[2 * slot + 1] = keys[slot, half:]
        value_rows[2 * slot, :, :HEAD] = values[slot, :half]
        value_rows[2 * slot + 1, :, :HEAD] = values[slot, half:]
    for part in range(2):
        for group in range(GROUPS):
            packed[part, group * half : (group + 1) * half, :] = queries[
                part * half : (part + 1) * half, group * HEAD : (group + 1) * HEAD
            ]
    best[...] = jnp.full(best.shape, LOW, jnp.float32)
    sums[...] = jnp.zeros(sums.shape, jnp.float32)
    splits = 2
    rows = stack // splits

    def visit(part, key_a, key_b, seen):
        key = jnp.concatenate([key_rows[key_a], key_rows[key_b]], axis=0)
        value = jnp.concatenate([value_rows[key_a], value_rows[key_b]], axis=0)
        for split in range(splits):
            at = pl.ds(split * rows, rows)
            score = lax.dot_general(
                packed[part, at, :], key, (((1,), (1,)), ((), ())), preferred_element_type=jnp.float32
            )
            if seen is not None:
                score = jnp.where(jnp.concatenate([seen] * (rows // half), axis=0), score, LOW)
            old = best[part, at, :]
            new = jnp.maximum(old, jnp.max(score, axis=1, keepdims=True))
            best[part, at, :] = new
            shrink = jnp.exp2((old - new) * scale)
            new_wide = jnp.concatenate([new] * (2 * half // HEAD), axis=1)
            weight = jnp.exp2((score - new_wide) * scale).astype(jnp.bfloat16)
            more = jnp.dot(weight, value, preferred_element_type=jnp.float32)
            sums[part, at, :] = sums[part, at, :] * jnp.concatenate([shrink, shrink], axis=1) + more

    for pair in range(count // 2):
        visit(1, 4 * pair, 4 * pair + 2, None)

    def dynamic(step, carry):
        entry = step * 8
        part, key_a, key_b = steps[entry], steps[entry + 1], steps[entry + 2]
        live = steps[entry + 7] == 1

        @pl.when(live & (steps[entry + 3] == 0))
        def _():
            visit(part, key_a, key_b, None)

        @pl.when(live & (steps[entry + 3] == 1))
        def _():
            lane = lax.broadcasted_iota(jnp.int32, (half, 2 * half), 1)
            row = lax.broadcasted_iota(jnp.int32, (half, 2 * half), 0)
            spot = jnp.where(lane < half, steps[entry + 5] + lane, steps[entry + 6] + lane - half)
            visit(part, key_a, key_b, spot <= steps[entry + 4] + row)

        return carry

    lax.fori_loop(0, pairs, dynamic, 0)
    for part in range(2):
        for group in range(GROUPS):
            at = pl.ds(group * half, half)
            out[part * half : (part + 1) * half, group * HEAD : (group + 1) * HEAD] = (
                sums[part, at, :HEAD] / sums[part, at, HEAD:]
            ).astype(out.dtype)


def attend(queries, shards, steps, pairs):
    tokens, width = queries.shape
    count = shards.shape[0]
    half = tokens // 2
    stack = GROUPS * half

    def body(*refs):
        attend_kernel(count, pairs, *refs)

    return pl.pallas_call(
        body,
        out_shape=jax.ShapeDtypeStruct((tokens, width), jnp.bfloat16),
        grid_spec=pltpu.PrefetchScalarGridSpec(
            num_scalar_prefetch=1,
            grid=(KV_HEADS,),
            in_specs=[
                pl.BlockSpec((tokens, GROUPS * HEAD), lambda h, s: (0, h)),
                pl.BlockSpec((count, tokens, HEAD), lambda h, s: (0, 0, h)),
                pl.BlockSpec((count, tokens, HEAD), lambda h, s: (0, 0, KV_HEADS + h)),
            ],
            out_specs=pl.BlockSpec((tokens, GROUPS * HEAD), lambda h, s: (0, h)),
            scratch_shapes=[
                pltpu.VMEM((2, stack, HEAD), jnp.bfloat16),
                pltpu.VMEM((2 * count, half, HEAD), jnp.bfloat16),
                pltpu.VMEM((2 * count, half, 2 * HEAD), jnp.bfloat16),
                pltpu.VMEM((2, stack, HEAD), jnp.float32),
                pltpu.VMEM((2, stack, 2 * HEAD), jnp.float32),
            ],
        ),
        compiler_params=pltpu.CompilerParams(vmem_limit_bytes=50 << 20),
        name="attend",
    )(steps, queries, shards, shards)


def shards(
    hidden, queries, weights_old, gradient_old, first_old, second_old, old_owner, new_owner, offsets
):
    devices = old_owner.shape[0]
    row_count, proj_width = weights_old.shape
    tok_rows = hidden.shape[1]
    half_tok = tok_rows // 2
    sizes = [lax.axis_size(a) for a in ALL]
    updated = adam_step(weights_old, gradient_old, first_old, second_old)
    copies = updated[0].astype(jnp.bfloat16)
    gathered = lax.all_gather(copies, TORUS, axis=0, tiled=False).reshape(
        devices, row_count, proj_width
    )
    owner_at = old_owner.reshape(sizes).transpose([ALL.index(a) for a in TORUS]).reshape(devices)
    source = invert(owner_at)
    moved = relocate(jnp.stack(updated), new_owner, old_owner)

    x_at, zl_at = lax.axis_index("x"), lax.axis_index("zl")
    pair = lax.axis_size("zl")
    table = offsets[0]
    mine = table[x_at * pair + zl_at]
    local = jnp.arange(tok_rows, dtype=jnp.int32)
    query_pos = jnp.where(local < half_tok, mine[0] + local, mine[1] + local - half_tok)
    exponent = jnp.arange(HEAD // 2, dtype=jnp.float32) * (2.0 / HEAD)
    inv_freq = jnp.power(rope_base, -exponent)
    angles = query_pos.astype(jnp.float32)[:, None] * inv_freq
    cosine, sine = jnp.cos(angles), jnp.sin(angles)
    cosine = jnp.concatenate([cosine, cosine], axis=1)
    sine = jnp.concatenate([-sine, sine], axis=1)

    both = table.reshape(lax.axis_size("x"), pair, 2)
    both = jnp.where(zl_at == 0, both, both[:, ::-1])
    steps = plan(mine, both.reshape(-1, 2), 5)

    gathered, source, cosine, sine, steps, moved = lax.optimization_barrier(
        (gathered, source, cosine, sine, steps, moved)
    )
    weights_new, first_new, second_new = (moved[0], moved[1], moved[2])
    rows_own = project(hidden[0], gathered, source, cosine, sine)
    swap = [(i, i ^ 1) for i in range(pair)]
    rows_near = lax.ppermute(rows_own, "zl", swap)
    near = jnp.stack([rows_own, rows_near])
    every = lax.all_gather(near, "x", axis=0, tiled=True)
    attended = attend(queries[0], every, steps, 5)
    return (weights_new, first_new, second_new, attended[None])


def solution(mesh):
    grid = Mesh(mesh.devices.reshape(2, 4, 2, 4, 2), ALL)
    in_specs = (
        P(DP, CTX, None),
        P(DP, CTX, None),
        P(ALL, None),
        P(ALL, None),
        P(ALL, None),
        P(ALL, None),
        P(),
        P(),
        P(DP, None, None),
    )
    out_specs = (
        P(ALL, None),
        P(ALL, None),
        P(ALL, None),
        P(DP, CTX, None),
    )
    return jax.shard_map(shards, mesh=grid, in_specs=in_specs, out_specs=out_specs, check_vma=False)
```

```python
import math

import jax
import jax.numpy as jnp
from jax import lax
from jax.experimental import pallas as pl
from jax.experimental.pallas import tpu as pltpu
from jax.sharding import Mesh
from jax.sharding import PartitionSpec as P

HEAD = 128
KV_HEADS = 4
Q_HEADS = 32
GROUPS = Q_HEADS // KV_HEADS
DP = ("zh", "y", "c")
CTX = ("x", "zl")
ALL = DP + CTX
TORUS = ("zh", "zl", "x", "y", "c")
HOLE = 1 << 20
LOW = -1e30


learn_rate = 0.0003
beta_one = 0.9
beta_two = 0.95
adam_eps = 1e-08
decay_rate = 0.1
step_number = 1000
corr_one = 1.0 - beta_one**step_number
corr_two = 1.0 - beta_two**step_number
rope_base = 500000.0


def in_blocks(value, dim, peers):
    before, after = (value.shape[:dim], value.shape[dim + 1 :])
    return jnp.moveaxis(value.reshape(*before, peers, -1, *after), dim, 0)


def adam_step(weights, gradient, first_mom, second_mom):
    first_next = beta_one * first_mom + (1.0 - beta_one) * gradient
    second_next = beta_two * second_mom + (1.0 - beta_two) * gradient * gradient
    direction = first_next / corr_one / (jnp.sqrt(second_next / corr_two) + adam_eps)
    weights_next = weights - learn_rate * (direction + decay_rate * weights)
    return (weights_next, first_next, second_next)


def invert(owners):
    devices = owners.shape[0]
    return jnp.zeros((devices,), jnp.int32).at[owners].set(jnp.arange(devices, dtype=jnp.int32))


def relocate(stacked, new_owner, old_owner):
    states_count, row_count, proj_width = stacked.shape
    devices = new_owner.shape[0]
    col_count = proj_width // devices
    outgoing = stacked.reshape(states_count, row_count, devices, col_count).transpose(2, 0, 3, 1)
    outgoing = jnp.take(outgoing, new_owner, axis=0)
    incoming = lax.all_to_all(outgoing, ALL, split_axis=0, concat_axis=0, tiled=True)
    ordered = jnp.take(incoming, invert(old_owner), axis=0)
    return ordered.transpose(1, 2, 0, 3).reshape(states_count, col_count, devices * row_count)


def project_kernel(source, hidden, gathered, cosine, sine, out, rows, cols, sums, row_sem, col_sem):
    blocks, block_rows, _ = gathered.shape
    tokens, width = hidden.shape
    chunks = row_sem.shape[0]
    per = blocks // chunks
    span = width // chunks

    def row_copy(block, chunk):
        return pltpu.make_async_copy(
            gathered.at[source[block]],
            rows.at[pl.ds(pl.multiple_of(block * block_rows, block_rows), block_rows)],
            row_sem.at[chunk],
        )

    def col_copy(chunk):
        return pltpu.make_async_copy(
            hidden.at[:, pl.ds(chunk * span, span)],
            cols.at[:, pl.ds(chunk * span, span)],
            col_sem.at[chunk],
        )

    for chunk in range(chunks):
        col_copy(chunk).start()

        def issue(i, carry, chunk=chunk):
            row_copy(chunk * per + i, chunk).start()
            return carry

        lax.fori_loop(0, per, issue, 0)
    for chunk in range(chunks):
        col_copy(chunk).wait()
        whole = rows.at[pl.ds(chunk * span, span)]
        pltpu.make_async_copy(whole, whole, row_sem.at[chunk]).wait()
        part = jnp.dot(
            cols[:, chunk * span : (chunk + 1) * span],
            rows[chunk * span : (chunk + 1) * span, :],
            preferred_element_type=jnp.float32,
        )
        if chunk == 0:
            sums[...] = part
        else:
            sums[...] += part
    for head in range(KV_HEADS):
        key = sums[:, head * HEAD : (head + 1) * HEAD]
        turned = pltpu.roll(key, HEAD // 2, 1)
        out[:, head * HEAD : (head + 1) * HEAD] = (
            key * cosine[...] + turned * sine[...]
        ).astype(out.dtype)
    key_width = KV_HEADS * HEAD
    out[:, key_width:] = sums[:, key_width:].astype(out.dtype)


def project(hidden, gathered, source, cosine, sine):
    tokens, width = hidden.shape
    blocks, block_rows, features = gathered.shape
    chunks = 8
    return pl.pallas_call(
        project_kernel,
        out_shape=jax.ShapeDtypeStruct((tokens, features), jnp.bfloat16),
        grid_spec=pltpu.PrefetchScalarGridSpec(
            num_scalar_prefetch=1,
            grid=(1,),
            in_specs=[
                pl.BlockSpec(memory_space=pltpu.HBM),
                pl.BlockSpec(memory_space=pltpu.HBM),
                pl.BlockSpec((tokens, HEAD), lambda i, s: (0, 0)),
                pl.BlockSpec((tokens, HEAD), lambda i, s: (0, 0)),
            ],
            out_specs=pl.BlockSpec((tokens, features), lambda i, s: (0, 0)),
            scratch_shapes=[
                pltpu.VMEM((width, features), jnp.bfloat16),
                pltpu.VMEM((tokens, width), jnp.bfloat16),
                pltpu.VMEM((tokens, features), jnp.float32),
                pltpu.SemaphoreType.DMA((chunks,)),
                pltpu.SemaphoreType.DMA((chunks,)),
            ],
        ),
        compiler_params=pltpu.CompilerParams(vmem_limit_bytes=44 << 20),
        name="project",
    )(source, hidden, gathered, cosine, sine)


def plan(mine, bases, pairs):
    count = bases.shape[0]
    low, high = bases[:, 0], bases[:, 1]
    own = low == mine[0]
    slots = jnp.arange(count, dtype=jnp.int32)
    has_own = jnp.any(own).astype(jnp.int32)

    def listed(chosen, segment, base):
        other = chosen & ~own
        earlier = jnp.sum(
            jnp.where((slots[None, :] < slots[:, None]) & other[None, :], 1, 0), axis=1
        )
        rank = jnp.where(own, 0, has_own + earlier)
        hit = chosen[None, :] & (rank[None, :] == jnp.arange(2 * pairs, dtype=jnp.int32)[:, None])
        found = jnp.any(hit, axis=1)
        keys = jnp.sum(jnp.where(hit, segment[None, :], 0), axis=1)
        starts = jnp.where(found, jnp.sum(jnp.where(hit, base[None, :], 0), axis=1), HOLE)
        return keys, starts, jnp.sum(jnp.where(chosen, 1, 0))

    low_keys, low_starts, low_count = listed(low <= mine[0], 2 * slots, low)
    high_keys, high_starts, high_count = listed(low >= mine[0], 2 * slots + 1, high)
    low_blocks = (low_count + 1) // 2
    high_blocks = (high_count + 1) // 2
    step = jnp.arange(pairs, dtype=jnp.int32)
    is_high = (step >= low_blocks).astype(jnp.int32)
    at = step - is_high * low_blocks
    take = jnp.arange(2 * pairs, dtype=jnp.int32)

    def pick(low_list, high_list, offset):
        one = take[None, :] == (2 * at + offset)[:, None]
        chosen = jnp.where(is_high[:, None] == 1, high_list[None, :], low_list[None, :])
        return jnp.sum(jnp.where(one, chosen, 0), axis=1)

    key_a, key_b = pick(low_keys, high_keys, 0), pick(low_keys, high_keys, 1)
    base_a, base_b = pick(low_starts, high_starts, 0), pick(low_starts, high_starts, 1)
    query_base = jnp.where(is_high == 1, mine[1], mine[0])
    masked = ((base_b == HOLE) | ((at == 0) & (has_own == 1))).astype(jnp.int32)
    live = (step < low_blocks + high_blocks).astype(jnp.int32)
    return jnp.stack(
        [is_high, key_a, key_b, masked, query_base, base_a, base_b, live], axis=1
    ).reshape(-1)


def attend_kernel(moves, segments, pairs, first, last, steps, queries, *refs):
    sources = len(moves)
    keys, values = refs[:sources], refs[sources : 2 * sources]
    rest = list(refs[2 * sources :])
    if not first:
        carried, packed_in = rest.pop(0), rest.pop(0)
    if last:
        out = rest.pop(0)
    else:
        kept, packed_out = rest.pop(0), rest.pop(0)
    packed, key_rows, value_rows, best, sums = rest
    half = queries.shape[0] // 2
    stack = GROUPS * half
    scale = math.log2(math.e) / math.sqrt(HEAD)

    @pl.when(pl.program_id(0) == 0)
    def _():
        value_rows[:, :, HEAD:] = jnp.ones((segments, half, HEAD), value_rows.dtype)

    for source, pieces in enumerate(moves):
        for start, segment, place, size in pieces:
            key_rows[segment, place : place + size] = keys[source][start : start + size]
            value_rows[segment, place : place + size, :HEAD] = values[source][start : start + size]
    for part in range(2):
        for group in range(GROUPS):
            packed[part, group * half : (group + 1) * half, :] = queries[
                part * half : (part + 1) * half, group * HEAD : (group + 1) * HEAD
            ]
    if first:
        best[...] = jnp.full(best.shape, LOW, jnp.float32)
        sums[...] = jnp.zeros(sums.shape, jnp.float32)
    else:
        for part in range(2):
            for group in range(GROUPS):
                at = pl.ds(group * half, half)
                top = packed_in[0, part, :, group : group + 1]
                total = packed_in[0, part, :, GROUPS + group : GROUPS + group + 1]
                best[part, at, :] = jnp.broadcast_to(top, (half, HEAD))
                sums[part, at, HEAD:] = jnp.broadcast_to(total, (half, HEAD))
                sums[part, at, :HEAD] = carried[0, part, at, :]
    splits = SPLITS
    rows = stack // splits

    def visit(part, key_a, key_b, seen):
        key = jnp.concatenate([key_rows[key_a], key_rows[key_b]], axis=0)
        value = jnp.concatenate([value_rows[key_a], value_rows[key_b]], axis=0)
        for split in range(splits):
            at = pl.ds(split * rows, rows)
            score = lax.dot_general(
                packed[part, at, :], key, (((1,), (1,)), ((), ())), preferred_element_type=jnp.float32
            )
            if seen is not None:
                score = jnp.where(jnp.concatenate([seen] * (rows // half), axis=0), score, LOW)
            old = best[part, at, :]
            new = jnp.maximum(old, jnp.max(score, axis=1, keepdims=True))
            best[part, at, :] = new
            shrink = jnp.exp2((old - new) * scale)
            new_wide = jnp.concatenate([new] * (2 * half // HEAD), axis=1)
            weight = jnp.exp2((score - new_wide) * scale).astype(jnp.bfloat16)
            more = jnp.dot(weight, value, preferred_element_type=jnp.float32)
            sums[part, at, :] = sums[part, at, :] * jnp.concatenate([shrink, shrink], axis=1) + more

    for pair in range(segments // 4):
        visit(1, 4 * pair, 4 * pair + 2, None)

    def dynamic(step, carry):
        entry = step * 8
        part, key_a, key_b = steps[entry], steps[entry + 1], steps[entry + 2]
        live = steps[entry + 7] == 1

        @pl.when(live & (steps[entry + 3] == 0))
        def _():
            visit(part, key_a, key_b, None)

        @pl.when(live & (steps[entry + 3] == 1))
        def _():
            lane = lax.broadcasted_iota(jnp.int32, (half, 2 * half), 1)
            row = lax.broadcasted_iota(jnp.int32, (half, 2 * half), 0)
            spot = jnp.where(lane < half, steps[entry + 5] + lane, steps[entry + 6] + lane - half)
            visit(part, key_a, key_b, spot <= steps[entry + 4] + row)

        return carry

    lax.fori_loop(0, pairs, dynamic, 0)
    lane = lax.broadcasted_iota(jnp.int32, (half, HEAD), 1)
    for part in range(2):
        table = jnp.zeros((half, HEAD), jnp.float32)
        for group in range(GROUPS):
            at = pl.ds(group * half, half)
            if last:
                out[part * half : (part + 1) * half, group * HEAD : (group + 1) * HEAD] = (
                    sums[part, at, :HEAD] / sums[part, at, HEAD:]
                ).astype(out.dtype)
            else:
                kept[0, part, at, :] = sums[part, at, :HEAD]
                table = jnp.where(lane == group, best[part, at, :], table)
                table = jnp.where(lane == GROUPS + group, sums[part, at, HEAD:], table)
        if not last:
            packed_out[0, part] = table


def attend(queries, arrays, moves, steps, pairs, carried=None, last=True):
    tokens, width = queries.shape
    half = tokens // 2
    stack = GROUPS * half
    segments = 1 + max(piece[1] for pieces in moves for piece in pieces)
    first = carried is None

    def body(*refs):
        attend_kernel(moves, segments, pairs, first, last, *refs)

    def column(offset):
        return [
            pl.BlockSpec((a.shape[0], HEAD), lambda h, s, offset=offset: (0, offset + h)) for a in arrays
        ]

    state_specs = [
        pl.BlockSpec((1, 2, stack, HEAD), lambda h, s: (h, 0, 0, 0)),
        pl.BlockSpec((1, 2, half, HEAD), lambda h, s: (h, 0, 0, 0)),
    ]
    wide = pl.BlockSpec((tokens, GROUPS * HEAD), lambda h, s: (0, h))
    if last:
        out_shape = jax.ShapeDtypeStruct((tokens, width), jnp.bfloat16)
        out_specs = wide
    else:
        out_shape = [
            pltpu.HBM((KV_HEADS, 2, stack, HEAD), jnp.float32),
            pltpu.HBM((KV_HEADS, 2, half, HEAD), jnp.float32),
        ]
        out_specs = state_specs
    if not first:
        carried = [pltpu.with_memory_space_constraint(a, pltpu.HBM) for a in carried]
    queries = pltpu.with_memory_space_constraint(queries, pltpu.HBM)
    return pl.pallas_call(
        body,
        out_shape=out_shape,
        grid_spec=pltpu.PrefetchScalarGridSpec(
            num_scalar_prefetch=1,
            grid=(KV_HEADS,),
            in_specs=[wide] + column(0) + column(KV_HEADS) + ([] if first else state_specs),
            out_specs=out_specs,
            scratch_shapes=[
                pltpu.VMEM((2, stack, HEAD), jnp.bfloat16),
                pltpu.VMEM((segments, half, HEAD), jnp.bfloat16),
                pltpu.VMEM((segments, half, 2 * HEAD), jnp.bfloat16),
                pltpu.VMEM((2, stack, HEAD), jnp.float32),
                pltpu.VMEM((2, stack, 2 * HEAD), jnp.float32),
            ],
        ),
        compiler_params=pltpu.CompilerParams(vmem_limit_bytes=40 << 20, flags=FLAGS),
        cost_estimate=pl.CostEstimate(
            flops=2 * 2 * Q_HEADS * (segments + 1) * half * half * HEAD * 2,
            transcendentals=Q_HEADS * (segments + 1) * half * half,
            bytes_accessed=30 << 20,
        ),
        name="attend_last" if last else "attend_first",
    )(steps, queries, *arrays, *arrays, *(() if first else carried))


SPLITS = 2
FLAGS = {}


def shards(
    hidden, queries, weights_old, gradient_old, first_old, second_old, old_owner, new_owner, offsets
):
    devices = old_owner.shape[0]
    row_count, proj_width = weights_old.shape
    tok_rows = hidden.shape[1]
    half_tok = tok_rows // 2
    sizes = [lax.axis_size(a) for a in ALL]
    updated = adam_step(weights_old, gradient_old, first_old, second_old)
    copies = updated[0].astype(jnp.bfloat16)
    gathered = lax.all_gather(copies, TORUS, axis=0, tiled=False).reshape(
        devices, row_count, proj_width
    )
    owner_at = old_owner.reshape(sizes).transpose([ALL.index(a) for a in TORUS]).reshape(devices)
    source = invert(owner_at)
    moved = relocate(jnp.stack(updated), new_owner, old_owner)

    x_at, zl_at = lax.axis_index("x"), lax.axis_index("zl")
    pair = lax.axis_size("zl")
    table = offsets[0]
    mine = table[x_at * pair + zl_at]
    local = jnp.arange(tok_rows, dtype=jnp.int32)
    query_pos = jnp.where(local < half_tok, mine[0] + local, mine[1] + local - half_tok)
    exponent = jnp.arange(HEAD // 2, dtype=jnp.float32) * (2.0 / HEAD)
    inv_freq = jnp.power(rope_base, -exponent)
    angles = query_pos.astype(jnp.float32)[:, None] * inv_freq
    cosine, sine = jnp.cos(angles), jnp.sin(angles)
    cosine = jnp.concatenate([cosine, cosine], axis=1)
    sine = jnp.concatenate([-sine, sine], axis=1)

    xs = lax.axis_size("x")
    order = [(0, 0), (0, 1), (-1, 0), (1, 0), (-1, 1), (1, 1), (2, 0), (2, 1)]
    places = jnp.stack([(x_at + dx) % xs * pair + (zl_at + dz) % pair for dx, dz in order])
    bases = jnp.take(table, places, axis=0)
    steps = jnp.stack([plan(mine, bases[:4], 3), plan(mine, bases[4:], 3)])

    gathered, source, cosine, sine, steps, moved = lax.optimization_barrier(
        (gathered, source, cosine, sine, steps, moved)
    )
    weights_new, first_new, second_new = (moved[0], moved[1], moved[2])
    in_hbm = pltpu.with_memory_space_constraint(hidden[0], pltpu.HBM)
    rows_own = project(in_hbm, gathered, source, cosine, sine)
    near = [(i, i ^ 1) for i in range(pair)]
    ahead = [(i, (i + 1) % xs) for i in range(xs)]
    behind = [(i, (i - 1) % xs) for i in range(xs)]
    lo, hi, quarter = slice(0, half_tok), slice(half_tok, None), half_tok // 2
    z_rows = lax.ppermute(rows_own, "zl", near)
    left = lax.ppermute(rows_own, "x", ahead)
    right = lax.ppermute(rows_own, "x", behind)
    left_lo = lax.ppermute(left[lo], "zl", near)
    left_hi = lax.ppermute(z_rows[hi], "x", ahead)
    right_hi = lax.ppermute(z_rows[hi], "x", behind)
    far_lo = lax.ppermute(left[lo], "x", ahead)
    far_hi = lax.ppermute(right[hi], "x", behind)
    right_lo = lax.ppermute(right[lo], "zl", near)
    whole = [(0, 0, 0, half_tok), (half_tok, 1, 0, half_tok)]
    state = attend(
        queries[0],
        [rows_own, z_rows, left, right],
        [[(start, 2 * i + seg, at, size) for start, seg, at, size in whole] for i in range(4)],
        steps[0],
        3,
        last=False,
    )
    left_lo, left_hi, right_lo, right_hi, far_lo, far_hi, state = lax.optimization_barrier(
        (left_lo, left_hi, right_lo, right_hi, far_lo, far_hi, state)
    )
    last_lo = lax.ppermute(far_lo, "zl", near)
    last_hi_a = lax.ppermute(left_hi[:quarter], "x", ahead)
    last_hi_b = lax.ppermute(right_hi[quarter:], "x", behind)
    pieces = [left_lo, left_hi, right_lo, right_hi, far_lo, far_hi, last_lo, last_hi_a, last_hi_b]
    moves = [[(0, i, 0, half_tok)] for i in range(7)]
    moves += [[(0, 7, 0, quarter)], [(0, 7, quarter, half_tok - quarter)]]
    attended = attend(queries[0], pieces, moves, steps[1], 3, carried=state)
    return (weights_new, first_new, second_new, attended[None])


def solution(mesh):
    grid = Mesh(mesh.devices.reshape(2, 4, 2, 4, 2), ALL)
    in_specs = (
        P(DP, CTX, None),
        P(DP, CTX, None),
        P(ALL, None),
        P(ALL, None),
        P(ALL, None),
        P(ALL, None),
        P(),
        P(),
        P(DP, None, None),
    )
    out_specs = (
        P(ALL, None),
        P(ALL, None),
        P(ALL, None),
        P(DP, CTX, None),
    )
    return jax.shard_map(shards, mesh=grid, in_specs=in_specs, out_specs=out_specs, check_vma=False)
```

```python
import math

import jax
import jax.numpy as jnp
from jax import lax
from jax.experimental import pallas as pl
from jax.experimental.pallas import tpu as pltpu
from jax.sharding import Mesh
from jax.sharding import PartitionSpec as P

HEAD = 128
KV_HEADS = 4
Q_HEADS = 32
GROUPS = Q_HEADS // KV_HEADS
DP = ("zh", "y", "c")
CTX = ("x", "zl")
ALL = DP + CTX
TORUS = ("zh", "zl", "x", "y", "c")
HOLE = 1 << 20
LOW = -1e30


learn_rate = 0.0003
beta_one = 0.9
beta_two = 0.95
adam_eps = 1e-08
decay_rate = 0.1
step_number = 1000
corr_one = 1.0 - beta_one**step_number
corr_two = 1.0 - beta_two**step_number
rope_base = 500000.0


def in_blocks(value, dim, peers):
    before, after = (value.shape[:dim], value.shape[dim + 1 :])
    return jnp.moveaxis(value.reshape(*before, peers, -1, *after), dim, 0)


def adam_step(weights, gradient, first_mom, second_mom):
    first_next = beta_one * first_mom + (1.0 - beta_one) * gradient
    second_next = beta_two * second_mom + (1.0 - beta_two) * gradient * gradient
    direction = first_next / corr_one / (jnp.sqrt(second_next / corr_two) + adam_eps)
    weights_next = weights - learn_rate * (direction + decay_rate * weights)
    return (weights_next, first_next, second_next)


def invert(owners):
    devices = owners.shape[0]
    return jnp.zeros((devices,), jnp.int32).at[owners].set(jnp.arange(devices, dtype=jnp.int32))


def relocate(stacked, new_owner, old_owner):
    states_count, row_count, proj_width = stacked.shape
    devices = new_owner.shape[0]
    col_count = proj_width // devices
    outgoing = stacked.reshape(states_count, row_count, devices, col_count).transpose(2, 0, 3, 1)
    outgoing = jnp.take(outgoing, new_owner, axis=0)
    incoming = lax.all_to_all(outgoing, ALL, split_axis=0, concat_axis=0, tiled=True)
    ordered = jnp.take(incoming, invert(old_owner), axis=0)
    return ordered.transpose(1, 2, 0, 3).reshape(states_count, col_count, devices * row_count)


def project_kernel(source, hidden, gathered, cosine, sine, out, rows, cols, sums, row_sem, col_sem):
    blocks, block_rows, _ = gathered.shape
    tokens, width = hidden.shape
    chunks = row_sem.shape[0]
    per = blocks // chunks
    span = width // chunks

    def row_copy(block, chunk):
        return pltpu.make_async_copy(
            gathered.at[source[block]],
            rows.at[pl.ds(pl.multiple_of(block * block_rows, block_rows), block_rows)],
            row_sem.at[chunk],
        )

    def col_copy(chunk):
        return pltpu.make_async_copy(
            hidden.at[:, pl.ds(chunk * span, span)],
            cols.at[:, pl.ds(chunk * span, span)],
            col_sem.at[chunk],
        )

    for chunk in range(chunks):
        col_copy(chunk).start()

        def issue(i, carry, chunk=chunk):
            row_copy(chunk * per + i, chunk).start()
            return carry

        lax.fori_loop(0, per, issue, 0)
    for chunk in range(chunks):
        col_copy(chunk).wait()
        whole = rows.at[pl.ds(chunk * span, span)]
        pltpu.make_async_copy(whole, whole, row_sem.at[chunk]).wait()
        part = jnp.dot(
            cols[:, chunk * span : (chunk + 1) * span],
            rows[chunk * span : (chunk + 1) * span, :],
            preferred_element_type=jnp.float32,
        )
        if chunk == 0:
            sums[...] = part
        else:
            sums[...] += part
    for head in range(KV_HEADS):
        key = sums[:, head * HEAD : (head + 1) * HEAD]
        turned = pltpu.roll(key, HEAD // 2, 1)
        out[:, head * HEAD : (head + 1) * HEAD] = (
            key * cosine[...] + turned * sine[...]
        ).astype(out.dtype)
    key_width = KV_HEADS * HEAD
    out[:, key_width:] = sums[:, key_width:].astype(out.dtype)


def project(hidden, gathered, source, cosine, sine):
    tokens, width = hidden.shape
    blocks, block_rows, features = gathered.shape
    chunks = 8
    return pl.pallas_call(
        project_kernel,
        out_shape=jax.ShapeDtypeStruct((tokens, features), jnp.bfloat16),
        grid_spec=pltpu.PrefetchScalarGridSpec(
            num_scalar_prefetch=1,
            grid=(1,),
            in_specs=[
                pl.BlockSpec(memory_space=pltpu.HBM),
                pl.BlockSpec(memory_space=pltpu.HBM),
                pl.BlockSpec((tokens, HEAD), lambda i, s: (0, 0)),
                pl.BlockSpec((tokens, HEAD), lambda i, s: (0, 0)),
            ],
            out_specs=pl.BlockSpec((tokens, features), lambda i, s: (0, 0)),
            scratch_shapes=[
                pltpu.VMEM((width, features), jnp.bfloat16),
                pltpu.VMEM((tokens, width), jnp.bfloat16),
                pltpu.VMEM((tokens, features), jnp.float32),
                pltpu.SemaphoreType.DMA((chunks,)),
                pltpu.SemaphoreType.DMA((chunks,)),
            ],
        ),
        compiler_params=pltpu.CompilerParams(vmem_limit_bytes=44 << 20),
        name="project",
    )(source, hidden, gathered, cosine, sine)


ENTRY = 5


def plan(mine, bases, pairs):
    count = bases.shape[0]
    low, high = bases[:, 0], bases[:, 1]
    own = low == mine[0]
    slots = jnp.arange(count, dtype=jnp.int32)
    has_own = jnp.any(own).astype(jnp.int32)
    wanted = jnp.arange(2 * pairs, dtype=jnp.int32)

    def listed(chosen, segment, reach):
        other = chosen & ~own
        earlier = jnp.sum(
            jnp.where((slots[None, :] < slots[:, None]) & other[None, :], 1, 0), axis=1
        )
        rank = jnp.where(own, 0, has_own + earlier)
        hit = chosen[None, :] & (rank[None, :] == wanted[:, None])
        found = jnp.any(hit, axis=1)
        keys = jnp.sum(jnp.where(hit, segment[None, :], 0), axis=1)
        reaches = jnp.where(found, jnp.sum(jnp.where(hit, reach[None, :], 0), axis=1), -HOLE)
        masked = (reaches[1::2] == -HOLE) | ((wanted[:pairs] == 0) & (has_own == 1))
        rows = jnp.stack(
            [keys[0::2], keys[1::2], masked.astype(jnp.int32), reaches[0::2], reaches[1::2]], axis=1
        )
        return (jnp.sum(jnp.where(chosen, 1, 0)) + 1) // 2, rows

    low_count, low_rows = listed(low <= mine[0], 2 * slots, mine[0] - low)
    high_count, high_rows = listed(low >= mine[0], 2 * slots + 1, mine[1] - high)
    fixed = jnp.asarray(
        [[4 * i, 4 * i + 2, 0, 0, 0] for i in range(count // 2)], jnp.int32
    )
    head = jnp.stack([low_count, high_count + count // 2])
    return jnp.concatenate([head, jnp.concatenate([low_rows, fixed, high_rows]).reshape(-1)])


def attend_kernel(moves, segments, pairs, first, last, steps, queries, *refs):
    sources = len(moves)
    keys, values = refs[:sources], refs[sources : 2 * sources]
    rest = list(refs[2 * sources :])
    if not first:
        carried, packed_in = rest.pop(0), rest.pop(0)
    if last:
        out = rest.pop(0)
    else:
        kept, packed_out = rest.pop(0), rest.pop(0)
    packed, key_rows, value_rows, delta = rest[:4]
    best, sums = rest[4:6], rest[6:8]
    half = queries.shape[0] // 2
    stack = GROUPS * half
    scale = math.log2(math.e) / math.sqrt(HEAD)
    span = SPAN

    @pl.when(pl.program_id(0) == 0)
    def _():
        lane = lax.broadcasted_iota(jnp.int32, delta.shape, 1)
        delta[...] = lax.broadcasted_iota(jnp.int32, delta.shape, 0) - lax.rem(lane, half)

    for source, pieces in enumerate(moves):
        for start, segment, place, size in pieces:
            key_rows[segment, place : place + size] = keys[source][start : start + size]
            value_rows[segment, place : place + size] = values[source][start : start + size]
    for part in range(2):
        for group in range(GROUPS):
            packed[part, group * half : (group + 1) * half, :] = queries[
                part * half : (part + 1) * half, group * HEAD : (group + 1) * HEAD
            ]
        if first:
            best[part][...] = jnp.full((1, stack), LOW, jnp.float32)
            sums[part][...] = jnp.zeros((HEAD + 8, stack), jnp.float32)
        else:
            best[part][...] = packed_in[0, part]
            sums[part][...] = carried[0, part]

    def visit(part, key_a, key_b, reach):
        key = jnp.concatenate([key_rows[key_a], key_rows[key_b]], axis=0)
        value = jnp.concatenate([value_rows[key_a], value_rows[key_b]], axis=0)
        turned = jnp.concatenate([value.T, jnp.ones((16, 2 * half), value.dtype)], axis=0)
        count = stack // span

        def raw(i):
            return lax.dot_general(
                key,
                packed[part, i * span : (i + 1) * span, :],
                (((1,), (1,)), ((), ())),
                preferred_element_type=jnp.float32,
            )

        scores = [raw(i) for i in range(min(AHEAD, count))]
        for i in range(count):
            at = slice(i * span, (i + 1) * span)
            score = scores[i]
            if reach is not None:
                gap = delta[:, at]
                seen = jnp.concatenate([gap <= reach[0], gap <= reach[1]], axis=0)
                score = jnp.where(seen, score, LOW)
            old = best[part][:, at]
            new = jnp.maximum(old, jnp.max(score, axis=0, keepdims=True))
            best[part][:, at] = new
            shrink = jnp.exp2((old - new) * scale)
            weight = jnp.exp2((score - new) * scale).astype(jnp.bfloat16)
            if i + AHEAD < count:
                scores.append(raw(i + AHEAD))
            more = jnp.dot(turned, weight, preferred_element_type=jnp.float32)
            sums[part][:, at] = sums[part][:, at] * shrink + more[: HEAD + 8]

    for part in range(2):
        begin = 2 + part * pairs * ENTRY

        def body(step, carry, part=part, begin=begin):
            entry = begin + step * ENTRY
            key_a, key_b = steps[entry], steps[entry + 1]

            @pl.when(steps[entry + 2] == 0)
            def _():
                visit(part, key_a, key_b, None)

            @pl.when(steps[entry + 2] == 1)
            def _():
                visit(part, key_a, key_b, (steps[entry + 3], steps[entry + 4]))

            return carry

        lax.fori_loop(0, steps[part], body, 0)
    for part in range(2):
        if not last:
            kept[0, part] = sums[part][...]
            packed_out[0, part] = best[part][...]
            continue
        for group in range(0, GROUPS, 2):
            at = slice(group * half, (group + 2) * half)
            done = (sums[part][:HEAD, at] / sums[part][HEAD : HEAD + 1, at]).T.astype(out.dtype)
            for side in range(2):
                out[
                    part * half : (part + 1) * half, (group + side) * HEAD : (group + side + 1) * HEAD
                ] = done[side * half : (side + 1) * half]


def attend(queries, arrays, moves, steps, pairs, carried=None, last=True):
    tokens, width = queries.shape
    half = tokens // 2
    stack = GROUPS * half
    segments = 1 + max(piece[1] for pieces in moves for piece in pieces)
    first = carried is None

    def body(*refs):
        attend_kernel(moves, segments, pairs, first, last, *refs)

    def column(offset):
        return [
            pl.BlockSpec((a.shape[0], HEAD), lambda h, s, offset=offset: (0, offset + h)) for a in arrays
        ]

    state_specs = [
        pl.BlockSpec((1, 2, HEAD + 8, stack), lambda h, s: (h, 0, 0, 0)),
        pl.BlockSpec((1, 2, 1, stack), lambda h, s: (h, 0, 0, 0)),
    ]
    wide = pl.BlockSpec((tokens, GROUPS * HEAD), lambda h, s: (0, h))
    if last:
        out_shape = jax.ShapeDtypeStruct((tokens, width), jnp.bfloat16)
        out_specs = wide
    else:
        out_shape = [
            pltpu.HBM((KV_HEADS, 2, HEAD + 8, stack), jnp.float32),
            pltpu.HBM((KV_HEADS, 2, 1, stack), jnp.float32),
        ]
        out_specs = state_specs
    if not first:
        carried = [pltpu.with_memory_space_constraint(a, pltpu.HBM) for a in carried]
    queries = pltpu.with_memory_space_constraint(queries, pltpu.HBM)
    return pl.pallas_call(
        body,
        out_shape=out_shape,
        grid_spec=pltpu.PrefetchScalarGridSpec(
            num_scalar_prefetch=1,
            grid=(KV_HEADS,),
            in_specs=[wide] + column(0) + column(KV_HEADS) + ([] if first else state_specs),
            out_specs=out_specs,
            scratch_shapes=[
                pltpu.VMEM((2, stack, HEAD), jnp.bfloat16),
                pltpu.VMEM((segments, half, HEAD), jnp.bfloat16),
                pltpu.VMEM((segments, half, HEAD), jnp.bfloat16),
                pltpu.VMEM((half, stack), jnp.int32),
                pltpu.VMEM((1, stack), jnp.float32),
                pltpu.VMEM((1, stack), jnp.float32),
                pltpu.VMEM((HEAD + 8, stack), jnp.float32),
                pltpu.VMEM((HEAD + 8, stack), jnp.float32),
            ],
        ),
        compiler_params=pltpu.CompilerParams(vmem_limit_bytes=40 << 20, flags=FLAGS),
        cost_estimate=pl.CostEstimate(
            flops=2 * 2 * Q_HEADS * (segments + 1) * half * half * HEAD * 2,
            transcendentals=Q_HEADS * (segments + 1) * half * half,
            bytes_accessed=30 << 20,
        ),
        name="attend_last" if last else "attend_first",
    )(steps, queries, *arrays, *arrays, *(() if first else carried))


SPAN = 512
AHEAD = 2
FLAGS = {}


def shards(
    hidden, queries, weights_old, gradient_old, first_old, second_old, old_owner, new_owner, offsets
):
    devices = old_owner.shape[0]
    row_count, proj_width = weights_old.shape
    tok_rows = hidden.shape[1]
    half_tok = tok_rows // 2
    sizes = [lax.axis_size(a) for a in ALL]
    updated = adam_step(weights_old, gradient_old, first_old, second_old)
    copies = updated[0].astype(jnp.bfloat16)
    gathered = lax.all_gather(copies, TORUS, axis=0, tiled=False).reshape(
        devices, row_count, proj_width
    )
    owner_at = old_owner.reshape(sizes).transpose([ALL.index(a) for a in TORUS]).reshape(devices)
    source = invert(owner_at)
    moved = relocate(jnp.stack(updated), new_owner, old_owner)

    x_at, zl_at = lax.axis_index("x"), lax.axis_index("zl")
    pair = lax.axis_size("zl")
    table = offsets[0]
    mine = table[x_at * pair + zl_at]
    local = jnp.arange(tok_rows, dtype=jnp.int32)
    query_pos = jnp.where(local < half_tok, mine[0] + local, mine[1] + local - half_tok)
    exponent = jnp.arange(HEAD // 2, dtype=jnp.float32) * (2.0 / HEAD)
    inv_freq = jnp.power(rope_base, -exponent)
    angles = query_pos.astype(jnp.float32)[:, None] * inv_freq
    cosine, sine = jnp.cos(angles), jnp.sin(angles)
    cosine = jnp.concatenate([cosine, cosine], axis=1)
    sine = jnp.concatenate([-sine, sine], axis=1)

    xs = lax.axis_size("x")
    order = [(0, 0), (0, 1), (-1, 0), (1, 0), (-1, 1), (1, 1), (2, 0), (2, 1)]
    places = jnp.stack([(x_at + dx) % xs * pair + (zl_at + dz) % pair for dx, dz in order])
    bases = jnp.take(table, places, axis=0)
    steps = jnp.stack([plan(mine, bases[:4], 3), plan(mine, bases[4:], 3)])

    gathered, source, cosine, sine, steps, moved = lax.optimization_barrier(
        (gathered, source, cosine, sine, steps, moved)
    )
    weights_new, first_new, second_new = (moved[0], moved[1], moved[2])
    in_hbm = pltpu.with_memory_space_constraint(hidden[0], pltpu.HBM)
    rows_own = project(in_hbm, gathered, source, cosine, sine)
    near = [(i, i ^ 1) for i in range(pair)]
    ahead = [(i, (i + 1) % xs) for i in range(xs)]
    behind = [(i, (i - 1) % xs) for i in range(xs)]
    z_rows = lax.ppermute(rows_own, "zl", near)
    left = lax.ppermute(rows_own, "x", ahead)
    right = lax.ppermute(rows_own, "x", behind)
    left_z = lax.ppermute(left, "zl", near)
    right_z = lax.ppermute(z_rows, "x", behind)
    far = lax.ppermute(left, "x", ahead)
    halves = [(0, 0, half_tok), (half_tok, 1, half_tok)]
    moves = [[(start, 2 * i + seg, 0, size) for start, seg, size in halves] for i in range(4)]
    state = attend(queries[0], [rows_own, z_rows, left, right], moves, steps[0], 3, last=False)
    left_z, right_z, far, state = lax.optimization_barrier((left_z, right_z, far, state))
    third = tok_rows // 3
    last_z = lax.ppermute(far[:third], "zl", near)
    last_left = lax.ppermute(left_z[third : 2 * third], "x", ahead)
    last_right = lax.ppermute(right_z[2 * third :], "x", behind)
    moves = moves[:3] + [
        [(0, 6, 0, third)],
        [(0, 6, third, half_tok - third), (half_tok - third, 7, 0, 2 * third - half_tok)],
        [(0, 7, 2 * third - half_tok, third)],
    ]
    attended = attend(
        queries[0], [left_z, right_z, far, last_z, last_left, last_right], moves, steps[1], 3, carried=state
    )
    return (weights_new, first_new, second_new, attended[None])


def solution(mesh):
    grid = Mesh(mesh.devices.reshape(2, 4, 2, 4, 2), ALL)
    in_specs = (
        P(DP, CTX, None),
        P(DP, CTX, None),
        P(ALL, None),
        P(ALL, None),
        P(ALL, None),
        P(ALL, None),
        P(),
        P(),
        P(DP, None, None),
    )
    out_specs = (
        P(ALL, None),
        P(ALL, None),
        P(ALL, None),
        P(DP, CTX, None),
    )
    return jax.shard_map(shards, mesh=grid, in_specs=in_specs, out_specs=out_specs, check_vma=False)
```

```python
import math

import jax
import jax.numpy as jnp
from jax import lax
from jax.experimental import pallas as pl
from jax.experimental.pallas import tpu as pltpu
from jax.sharding import Mesh
from jax.sharding import PartitionSpec as P

HEAD = 128
KV_HEADS = 4
Q_HEADS = 32
GROUPS = Q_HEADS // KV_HEADS
DP = ("zh", "y", "c")
CTX = ("x", "zl")
ALL = DP + CTX
TORUS = ("zh", "zl", "x", "y", "c")
HOLE = 1 << 20
LOW = -1e30


learn_rate = 0.0003
beta_one = 0.9
beta_two = 0.95
adam_eps = 1e-08
decay_rate = 0.1
step_number = 1000
corr_one = 1.0 - beta_one**step_number
corr_two = 1.0 - beta_two**step_number
rope_base = 500000.0


def in_blocks(value, dim, peers):
    before, after = (value.shape[:dim], value.shape[dim + 1 :])
    return jnp.moveaxis(value.reshape(*before, peers, -1, *after), dim, 0)


def adam_step(weights, gradient, first_mom, second_mom):
    first_next = beta_one * first_mom + (1.0 - beta_one) * gradient
    second_next = beta_two * second_mom + (1.0 - beta_two) * gradient * gradient
    direction = first_next / corr_one / (jnp.sqrt(second_next / corr_two) + adam_eps)
    weights_next = weights - learn_rate * (direction + decay_rate * weights)
    return (weights_next, first_next, second_next)


def invert(owners):
    devices = owners.shape[0]
    return jnp.zeros((devices,), jnp.int32).at[owners].set(jnp.arange(devices, dtype=jnp.int32))


def relocate(stacked, new_owner, old_owner):
    states_count, row_count, proj_width = stacked.shape
    devices = new_owner.shape[0]
    col_count = proj_width // devices
    outgoing = stacked.reshape(states_count, row_count, devices, col_count).transpose(2, 0, 3, 1)
    outgoing = jnp.take(outgoing, new_owner, axis=0)
    incoming = lax.all_to_all(outgoing, ALL, split_axis=0, concat_axis=0, tiled=True)
    ordered = jnp.take(incoming, invert(old_owner), axis=0)
    return ordered.transpose(1, 2, 0, 3).reshape(states_count, col_count, devices * row_count)


def project_kernel(source, hidden, gathered, cosine, sine, out, rows, cols, sums, row_sem, col_sem):
    blocks, block_rows, _ = gathered.shape
    tokens, width = hidden.shape
    chunks = row_sem.shape[0]
    per = blocks // chunks
    span = width // chunks

    def row_copy(block, chunk):
        return pltpu.make_async_copy(
            gathered.at[source[block]],
            rows.at[pl.ds(pl.multiple_of(block * block_rows, block_rows), block_rows)],
            row_sem.at[chunk],
        )

    def col_copy(chunk):
        return pltpu.make_async_copy(
            hidden.at[:, pl.ds(chunk * span, span)],
            cols.at[:, pl.ds(chunk * span, span)],
            col_sem.at[chunk],
        )

    for chunk in range(chunks):
        col_copy(chunk).start()

        def issue(i, carry, chunk=chunk):
            row_copy(chunk * per + i, chunk).start()
            return carry

        lax.fori_loop(0, per, issue, 0)
    for chunk in range(chunks):
        col_copy(chunk).wait()
        whole = rows.at[pl.ds(chunk * span, span)]
        pltpu.make_async_copy(whole, whole, row_sem.at[chunk]).wait()
        part = jnp.dot(
            cols[:, chunk * span : (chunk + 1) * span],
            rows[chunk * span : (chunk + 1) * span, :],
            preferred_element_type=jnp.float32,
        )
        if chunk == 0:
            sums[...] = part
        else:
            sums[...] += part
    for head in range(KV_HEADS):
        key = sums[:, head * HEAD : (head + 1) * HEAD]
        turned = pltpu.roll(key, HEAD // 2, 1)
        out[:, head * HEAD : (head + 1) * HEAD] = (
            key * cosine[...] + turned * sine[...]
        ).astype(out.dtype)
    key_width = KV_HEADS * HEAD
    out[:, key_width:] = sums[:, key_width:].astype(out.dtype)


def project(hidden, gathered, source, cosine, sine):
    tokens, width = hidden.shape
    blocks, block_rows, features = gathered.shape
    chunks = 8
    return pl.pallas_call(
        project_kernel,
        out_shape=jax.ShapeDtypeStruct((tokens, features), jnp.bfloat16),
        grid_spec=pltpu.PrefetchScalarGridSpec(
            num_scalar_prefetch=1,
            grid=(1,),
            in_specs=[
                pl.BlockSpec(memory_space=pltpu.HBM),
                pl.BlockSpec(memory_space=pltpu.HBM),
                pl.BlockSpec((tokens, HEAD), lambda i, s: (0, 0)),
                pl.BlockSpec((tokens, HEAD), lambda i, s: (0, 0)),
            ],
            out_specs=pl.BlockSpec((tokens, features), lambda i, s: (0, 0)),
            scratch_shapes=[
                pltpu.VMEM((width, features), jnp.bfloat16),
                pltpu.VMEM((tokens, width), jnp.bfloat16),
                pltpu.VMEM((tokens, features), jnp.float32),
                pltpu.SemaphoreType.DMA((chunks,)),
                pltpu.SemaphoreType.DMA((chunks,)),
            ],
        ),
        compiler_params=pltpu.CompilerParams(vmem_limit_bytes=44 << 20),
        name="project",
    )(source, hidden, gathered, cosine, sine)


ENTRY = 5


def plan(mine, bases, mine_first):
    skip = int(mine_first)
    count = bases.shape[0]
    low = bases[skip:, 0]
    others = count - skip
    slots = jnp.arange(others, dtype=jnp.int32)
    under = low < mine[0]
    wanted = jnp.arange(2 * count, dtype=jnp.int32)

    def listed(chosen, segment):
        earlier = (slots[None, :] < slots[:, None]) & chosen[None, :]
        rank = jnp.sum(jnp.where(earlier, 1, 0), axis=1)
        hit = chosen[None, :] & (rank[None, :] == wanted[:, None])
        return jnp.sum(jnp.where(hit, segment[None, :], 0), axis=1)

    lows = listed(under, 2 * (slots + skip))
    highs = listed(~under, 2 * (slots + skip) + 1)
    low_count = jnp.sum(jnp.where(under, 1, 0))
    high_count = 2 * others - low_count
    if mine_first:
        first_hole = jnp.where(low_count == 0, 1, 0)
        first_key = lows[0]
        lows = jnp.concatenate([lows[1:], lows[:1]])
        low_count = jnp.maximum(low_count - 1, 0)
    highs = jnp.concatenate([2 * (slots + skip), highs])[: 2 * count]
    step = jnp.arange(STEPS - 2 * skip, dtype=jnp.int32)
    low_full, high_full = low_count // 2, high_count // 2
    low_odd, high_odd = low_count % 2, high_count % 2
    after = step - low_full - high_full
    in_low = step < low_full
    in_high = ~in_low & (after < 0)
    end_low = (after == 0) & (low_odd == 1)
    end_high = (after == low_odd) & (high_odd == 1)
    half = jnp.where(in_low | end_low, 0, 1)
    at = jnp.where(in_low, 2 * step, 2 * (step - low_full))
    at = jnp.where(end_low, low_count - 1, jnp.where(end_high, high_count - 1, at))
    full = in_low | in_high

    def pick(index):
        one = wanted[None, :] == index[:, None]
        chosen = jnp.where(half[:, None] == 0, lows[None, :], highs[None, :])
        return jnp.sum(jnp.where(one, chosen, 0), axis=1)

    hole_a = jnp.where(full | end_low | end_high, 0, 1)
    rows = jnp.stack([half, pick(at), pick(at + 1), hole_a, jnp.where(full, 0, 1)], axis=1)
    if mine_first:
        zero = jnp.zeros((), jnp.int32)
        fixed = jnp.stack(
            [zero, zero, first_key, zero, first_hole, zero + 1, zero + 1, zero, zero, zero]
        )
        return jnp.concatenate([fixed, rows.reshape(-1)])
    return rows.reshape(-1)


def attend_kernel(moves, first, last, steps, queries, *refs):
    sources = len(moves)
    keys, values = refs[:sources], refs[sources : 2 * sources]
    rest = list(refs[2 * sources :])
    if not first:
        carried, packed_in = rest.pop(0), rest.pop(0)
    if last:
        out = rest.pop(0)
    else:
        kept, packed_out = rest.pop(0), rest.pop(0)
    packed, key_rows, value_rows, corner, best, sums = rest
    half = queries.shape[0] // 2
    stack = GROUPS * half
    scale = math.log2(math.e) / math.sqrt(HEAD)
    span = SPAN
    chunks = stack // span

    if first:

        @pl.when(pl.program_id(0) == 0)
        def _():
            lane = lax.broadcasted_iota(jnp.int32, corner.shape, 1)
            row = lax.broadcasted_iota(jnp.int32, corner.shape, 0)
            corner[...] = jnp.where(row <= lax.rem(lane, half), 0.0, LOW)

    for source, pieces in enumerate(moves):
        for start, segment, place, size in pieces:
            key_rows[segment, place : place + size] = keys[source][start : start + size]
            value_rows[segment, place : place + size] = values[source][start : start + size]
    for part in range(2):
        for group in range(GROUPS):
            packed[part, group * half : (group + 1) * half, :] = queries[
                part * half : (part + 1) * half, group * HEAD : (group + 1) * HEAD
            ]
    if not first:
        best[...] = packed_in[0]
        sums[...] = carried[0]

    seen = []
    for step in range(STEPS):
        entry = step * ENTRY
        fresh = first and step < 2
        part = step if fresh else steps[entry]
        key_a, key_b = steps[entry + 1], steps[entry + 2]
        key = jnp.concatenate([key_rows[key_a], key_rows[key_b]], axis=0)
        value = jnp.concatenate([value_rows[key_a], value_rows[key_b]], axis=0)
        turned = jnp.concatenate([value.T, jnp.ones((16, 2 * half), value.dtype)], axis=0)
        seen.append((entry, fresh, part, key, turned))

    def raw(unit):
        _, _, part, key, _ = seen[unit // chunks]
        at = unit % chunks * span
        return lax.dot_general(
            key, packed[part, at : at + span, :], (((1,), (1,)), ((), ())), preferred_element_type=jnp.float32
        )

    units = STEPS * chunks
    scores = [raw(unit) for unit in range(AHEAD)]
    for unit in range(units):
        step = unit // chunks
        entry, fresh, part, key, turned = seen[step]
        at = slice(unit % chunks * span, (unit % chunks + 1) * span)
        score = scores[unit]
        scores[unit] = None
        upper, lower = score[:half], score[half:]
        if fresh:
            upper = upper + corner[:, at]
        if not first and step == STEPS - 1:
            upper = upper + jnp.where(steps[entry + 3] == 1, LOW, 0.0)
        if (first and step in (0, STEPS - 1)) or (not first and step >= STEPS - 2):
            lower = lower + jnp.where(steps[entry + 4] == 1, LOW, 0.0)
        score = jnp.concatenate([upper, lower], axis=0)
        new = jnp.max(score, axis=0, keepdims=True)
        if not fresh:
            old = best[part, :, at]
            new = jnp.maximum(old, new)
        best[part, :, at] = new
        weight = jnp.exp2((score - new) * scale).astype(jnp.bfloat16)
        if unit + AHEAD < units:
            scores.append(raw(unit + AHEAD))
        more = jnp.dot(turned, weight, preferred_element_type=jnp.float32)[: HEAD + 8]
        if not fresh:
            more = sums[part, :, at] * jnp.exp2((old - new) * scale) + more
        sums[part, :, at] = more

    if not last:
        kept[0] = sums[...]
        packed_out[0] = best[...]
        return
    for part in range(2):
        for group in range(0, GROUPS, 2):
            at = slice(group * half, (group + 2) * half)
            done = (sums[part, :HEAD, at] / sums[part, HEAD : HEAD + 1, at]).T.astype(out.dtype)
            for side in range(2):
                out[
                    part * half : (part + 1) * half, (group + side) * HEAD : (group + side + 1) * HEAD
                ] = done[side * half : (side + 1) * half]


def attend(queries, arrays, moves, steps, carried=None, last=True):
    tokens, width = queries.shape
    half = tokens // 2
    stack = GROUPS * half
    segments = 1 + max(piece[1] for pieces in moves for piece in pieces)
    first = carried is None

    def body(*refs):
        attend_kernel(moves, first, last, *refs)

    def column(offset):
        return [
            pl.BlockSpec((a.shape[0], HEAD), lambda h, s, offset=offset: (0, offset + h)) for a in arrays
        ]

    state_specs = [
        pl.BlockSpec((1, 2, HEAD + 8, stack), lambda h, s: (h, 0, 0, 0)),
        pl.BlockSpec((1, 2, 1, stack), lambda h, s: (h, 0, 0, 0)),
    ]
    wide = pl.BlockSpec((tokens, GROUPS * HEAD), lambda h, s: (0, h))
    if last:
        out_shape = jax.ShapeDtypeStruct((tokens, width), jnp.bfloat16)
        out_specs = wide
    else:
        out_shape = [
            pltpu.HBM((KV_HEADS, 2, HEAD + 8, stack), jnp.float32),
            pltpu.HBM((KV_HEADS, 2, 1, stack), jnp.float32),
        ]
        out_specs = state_specs
    if not first:
        carried = [pltpu.with_memory_space_constraint(a, pltpu.HBM) for a in carried]
    queries = pltpu.with_memory_space_constraint(queries, pltpu.HBM)
    return pl.pallas_call(
        body,
        out_shape=out_shape,
        grid_spec=pltpu.PrefetchScalarGridSpec(
            num_scalar_prefetch=1,
            grid=(KV_HEADS,),
            in_specs=[wide] + column(0) + column(KV_HEADS) + ([] if first else state_specs),
            out_specs=out_specs,
            scratch_shapes=[
                pltpu.VMEM((2, stack, HEAD), jnp.bfloat16),
                pltpu.VMEM((segments, half, HEAD), jnp.bfloat16),
                pltpu.VMEM((segments, half, HEAD), jnp.bfloat16),
                pltpu.VMEM((half, stack), jnp.float32),
                pltpu.VMEM((2, 1, stack), jnp.float32),
                pltpu.VMEM((2, HEAD + 8, stack), jnp.float32),
            ],
        ),
        compiler_params=pltpu.CompilerParams(vmem_limit_bytes=40 << 20, flags=FLAGS),
        cost_estimate=pl.CostEstimate(
            flops=2 * 2 * Q_HEADS * (segments + 1) * half * half * HEAD * 2,
            transcendentals=Q_HEADS * (segments + 1) * half * half,
            bytes_accessed=30 << 20,
        ),
        name="attend_last" if last else "attend_first",
    )(steps, queries, *arrays, *arrays, *(() if first else carried))


SPAN = 512
STEPS = 5
AHEAD = 2
FLAGS = {}


def shards(
    hidden, queries, weights_old, gradient_old, first_old, second_old, old_owner, new_owner, offsets
):
    devices = old_owner.shape[0]
    row_count, proj_width = weights_old.shape
    tok_rows = hidden.shape[1]
    half_tok = tok_rows // 2
    sizes = [lax.axis_size(a) for a in ALL]
    updated = adam_step(weights_old, gradient_old, first_old, second_old)
    copies = updated[0].astype(jnp.bfloat16)
    gathered = lax.all_gather(copies, TORUS, axis=0, tiled=False).reshape(
        devices, row_count, proj_width
    )
    owner_at = old_owner.reshape(sizes).transpose([ALL.index(a) for a in TORUS]).reshape(devices)
    source = invert(owner_at)
    moved = relocate(jnp.stack(updated), new_owner, old_owner)

    x_at, zl_at = lax.axis_index("x"), lax.axis_index("zl")
    pair = lax.axis_size("zl")
    table = offsets[0]
    mine = table[x_at * pair + zl_at]
    local = jnp.arange(tok_rows, dtype=jnp.int32)
    query_pos = jnp.where(local < half_tok, mine[0] + local, mine[1] + local - half_tok)
    exponent = jnp.arange(HEAD // 2, dtype=jnp.float32) * (2.0 / HEAD)
    inv_freq = jnp.power(rope_base, -exponent)
    angles = query_pos.astype(jnp.float32)[:, None] * inv_freq
    cosine, sine = jnp.cos(angles), jnp.sin(angles)
    cosine = jnp.concatenate([cosine, cosine], axis=1)
    sine = jnp.concatenate([-sine, sine], axis=1)

    xs = lax.axis_size("x")
    order = [(0, 0), (0, 1), (-1, 0), (1, 0), (-1, 1), (1, 1), (2, 0), (2, 1)]
    places = jnp.stack([(x_at + dx) % xs * pair + (zl_at + dz) % pair for dx, dz in order])
    bases = jnp.take(table, places, axis=0)
    steps = jnp.stack([plan(mine, bases[:4], True), plan(mine, bases[4:], False)])

    gathered, source, cosine, sine, steps, moved = lax.optimization_barrier(
        (gathered, source, cosine, sine, steps, moved)
    )
    weights_new, first_new, second_new = (moved[0], moved[1], moved[2])
    in_hbm = pltpu.with_memory_space_constraint(hidden[0], pltpu.HBM)
    rows_own = project(in_hbm, gathered, source, cosine, sine)
    near = [(i, i ^ 1) for i in range(pair)]
    ahead = [(i, (i + 1) % xs) for i in range(xs)]
    behind = [(i, (i - 1) % xs) for i in range(xs)]
    z_rows = lax.ppermute(rows_own, "zl", near)
    left = lax.ppermute(rows_own, "x", ahead)
    right = lax.ppermute(rows_own, "x", behind)
    left_z = lax.ppermute(left, "zl", near)
    right_z = lax.ppermute(z_rows, "x", behind)
    far = lax.ppermute(left, "x", ahead)
    halves = [(0, 0, half_tok), (half_tok, 1, half_tok)]
    moves = [[(start, 2 * i + seg, 0, size) for start, seg, size in halves] for i in range(4)]
    state = attend(queries[0], [rows_own, z_rows, left, right], moves, steps[0], last=False)
    left_z, right_z, far, state = lax.optimization_barrier((left_z, right_z, far, state))
    third = tok_rows // 3
    last_z = lax.ppermute(far[:third], "zl", near)
    last_left = lax.ppermute(left_z[third : 2 * third], "x", ahead)
    last_right = lax.ppermute(right_z[2 * third :], "x", behind)
    moves = moves[:3] + [
        [(0, 6, 0, third)],
        [(0, 6, third, half_tok - third), (half_tok - third, 7, 0, 2 * third - half_tok)],
        [(0, 7, 2 * third - half_tok, third)],
    ]
    attended = attend(
        queries[0], [left_z, right_z, far, last_z, last_left, last_right], moves, steps[1], carried=state
    )
    return (weights_new, first_new, second_new, attended[None])


def solution(mesh):
    grid = Mesh(mesh.devices.reshape(2, 4, 2, 4, 2), ALL)
    in_specs = (
        P(DP, CTX, None),
        P(DP, CTX, None),
        P(ALL, None),
        P(ALL, None),
        P(ALL, None),
        P(ALL, None),
        P(),
        P(),
        P(DP, None, None),
    )
    out_specs = (
        P(ALL, None),
        P(ALL, None),
        P(ALL, None),
        P(DP, CTX, None),
    )
    return jax.shard_map(shards, mesh=grid, in_specs=in_specs, out_specs=out_specs, check_vma=False)
```

```python
import math

import jax
import jax.numpy as jnp
from jax import lax
from jax.experimental import pallas as pl
from jax.experimental.pallas import tpu as pltpu
from jax.sharding import Mesh
from jax.sharding import PartitionSpec as P


HEAD = 128
KV_HEADS = 4
Q_HEADS = 32
GROUPS = Q_HEADS // KV_HEADS
DP = ("zh", "y", "c")
CTX = ("x", "zl")
ALL = DP + CTX
LOW = -1e30


learn_rate = 0.0003
beta_one = 0.9
beta_two = 0.95
adam_eps = 1e-08
decay_rate = 0.1
step_number = 1000
corr_one = 1.0 - beta_one**step_number
corr_two = 1.0 - beta_two**step_number
rope_base = 500000.0


def adam_step(weights, gradient, first_mom, second_mom):
    first_next = beta_one * first_mom + (1.0 - beta_one) * gradient
    second_next = beta_two * second_mom + (1.0 - beta_two) * gradient * gradient
    direction = first_next / corr_one / (jnp.sqrt(second_next / corr_two) + adam_eps)
    weights_next = weights - learn_rate * (direction + decay_rate * weights)
    return (weights_next, first_next, second_next)


def invert(owners):
    devices = owners.shape[0]
    return jnp.zeros((devices,), jnp.int32).at[owners].set(jnp.arange(devices, dtype=jnp.int32))


def relocate(stacked, new_owner, old_owner):
    states_count, row_count, proj_width = stacked.shape
    devices = new_owner.shape[0]
    col_count = proj_width // devices
    outgoing = stacked.reshape(states_count, row_count, devices, col_count).transpose(2, 0, 3, 1)
    outgoing = jnp.take(outgoing, new_owner, axis=0)
    incoming = lax.all_to_all(outgoing, ALL, split_axis=0, concat_axis=0, tiled=True)
    ordered = jnp.take(incoming, invert(old_owner), axis=0)
    return ordered.transpose(1, 2, 0, 3).reshape(states_count, col_count, devices * row_count)


def ring(value, axis, distance):
    size = lax.axis_size(axis)
    return lax.ppermute(value, axis, [(i, (i + distance) % size) for i in range(size)])


def around(value, axis):
    return jnp.concatenate(
        [value, ring(value, axis, 1), ring(value, axis, -1), ring(value, axis, 2)], axis=0
    )


def around_last(value, axis):
    half = value.shape[0] // 2
    below = ring(value, axis, 1)
    above = ring(value, axis, -1)
    return [value, below, above, ring(below[:half], axis, 1), ring(above[half:], axis, -1)]


OFFSETS = (0, -1, 1, 2)
DEPTH = ("zh", "zl")
ORDERS = ((DEPTH, "x", "y"), ("x", "y", DEPTH), ("y", DEPTH, "x"))
PARTS = ((0, 384), (384, 768), (768, 1024))


def column_kernel(blocks, hidden, out):
    tiles = out.shape[2] // HEAD
    half = HEAD // 2
    base = (pl.program_id(0) * pl.num_programs(1) + pl.program_id(1)) * tiles * 2
    row = lax.broadcasted_iota(jnp.int32, (2 * HEAD, HEAD), 0)
    lane = lax.broadcasted_iota(jnp.int32, (2 * HEAD, HEAD), 1)
    for tile in range(tiles):
        left, right = blocks[base + 2 * tile], blocks[base + 2 * tile + 1]
        pair = jnp.concatenate(
            [
                hidden[:, pl.ds(pl.multiple_of(left // 2 * HEAD, HEAD), HEAD)],
                hidden[:, pl.ds(pl.multiple_of(right // 2 * HEAD, HEAD), HEAD)],
            ],
            axis=1,
        )
        wanted = jnp.where(
            lane < half, left % 2 * half + lane, HEAD + right % 2 * half + lane - half
        )
        choose = jnp.where(row == wanted, 1.0, 0.0).astype(hidden.dtype)
        out[0, :, tile * HEAD : (tile + 1) * HEAD] = jnp.dot(
            pair, choose, preferred_element_type=jnp.float32
        ).astype(out.dtype)


def choose_columns(hidden, blocks):
    tokens, width = hidden.shape
    steps, span = 4, width // 2 // 4
    return pl.pallas_call(
        column_kernel,
        out_shape=pltpu.HBM((2, tokens, width // 2), hidden.dtype),
        grid_spec=pltpu.PrefetchScalarGridSpec(
            num_scalar_prefetch=1,
            grid=(2, steps),
            in_specs=[pl.BlockSpec((tokens, width), lambda i, j, b: (0, 0))],
            out_specs=pl.BlockSpec((1, tokens, span), lambda i, j, b: (i, 0, j)),
        ),
        compiler_params=pltpu.CompilerParams(vmem_limit_bytes=24 << 20),
        name="columns",
    )(blocks, pltpu.with_memory_space_constraint(hidden, pltpu.HBM))


def partial_kernel(theirs, ours, *refs):
    count = len(OFFSETS)
    sources = [refs[5 * part : 5 * part + 5] for part in range(3)]
    outs, (rows, cols, first_sem, row_sem, col_sem) = refs[15:17], refs[17:]
    hiddens = (theirs, ours)
    span = theirs.shape[1] // count

    def tiles(part, third):
        if third < count - 1:
            return [(sources[part][third].at[i], i) for i in range(count)]
        low, high = sources[part][3], sources[part][4]
        return [(low.at[i], i) for i in range(2)] + [(high.at[i], 2 + i) for i in range(2)]

    def columns(part):
        return pl.ds(PARTS[part][0], PARTS[part][1] - PARTS[part][0])

    for y in range(count):
        for tile, x in tiles(0, y):
            pltpu.make_async_copy(tile, rows.at[:, x, y, :, columns(0)], first_sem).start()
    for z in range(count):
        for side in range(2):
            pltpu.make_async_copy(
                hiddens[side].at[:, pl.ds(z * span, span)], cols.at[z, side], col_sem.at[z]
            ).start()
        for tile, y in tiles(1, z):
            pltpu.make_async_copy(tile, rows.at[z, :, y, :, columns(1)], row_sem.at[z]).start()
        for x in range(count):
            for tile, at in tiles(2, x):
                if at == z:
                    pltpu.make_async_copy(tile, rows.at[z, x, :, :, columns(2)], row_sem.at[z]).start()
    for out in outs:
        out[...] = jnp.zeros(out.shape, out.dtype)
    whole = rows.at[:, :, :, :, columns(0)]
    pltpu.make_async_copy(whole, whole, first_sem).wait()

    def step(z, carry):
        piece = cols.at[z]
        pltpu.make_async_copy(piece, piece, col_sem.at[z]).wait()
        rest = rows.at[z, :, :, :, pl.ds(PARTS[1][0], PARTS[2][1] - PARTS[1][0])]
        pltpu.make_async_copy(rest, rest, row_sem.at[z]).wait()
        tokens = cols.shape[2]
        part = jnp.dot(
            cols[z].reshape(2 * tokens, span),
            rows[z].reshape(span, rows.shape[-1]),
            preferred_element_type=jnp.float32,
        )
        for side in range(2):
            outs[side][...] += part[side * tokens : (side + 1) * tokens]
        return carry

    lax.fori_loop(0, count, step, 0)


def partial_products(theirs, ours, arrays):
    tokens, width = ours.shape
    features = PARTS[-1][1]
    count = len(OFFSETS)
    size = width // count**3
    arrays = [a.reshape(-1, count, size, a.shape[-1]) for a in arrays]
    in_vmem = pl.BlockSpec(memory_space=pltpu.VMEM)
    return pl.pallas_call(
        partial_kernel,
        out_shape=[jax.ShapeDtypeStruct((tokens, features), jnp.float32)] * 2,
        in_specs=[pl.BlockSpec(memory_space=pl.ANY) for _ in range(17)],
        out_specs=[in_vmem, in_vmem],
        scratch_shapes=[
            pltpu.VMEM((count, count, count, size, features), jnp.bfloat16),
            pltpu.VMEM((count, 2, tokens, width // count), jnp.bfloat16),
            pltpu.SemaphoreType.DMA,
            pltpu.SemaphoreType.DMA((count,)),
            pltpu.SemaphoreType.DMA((count,)),
        ],
        compiler_params=pltpu.CompilerParams(vmem_limit_bytes=30 << 20),
        cost_estimate=pl.CostEstimate(
            flops=4 * tokens * width * features, transcendentals=0, bytes_accessed=18 << 20
        ),
        name="partial",
    )(theirs, ours, *arrays)


def finish_kernel(own, other, cosine, sine, out):
    key_width = KV_HEADS * HEAD
    for head in range(KV_HEADS):
        at = slice(head * HEAD, (head + 1) * HEAD)
        key = own[:, at] + other[:, at]
        turned = pltpu.roll(key, HEAD // 2, 1)
        out[:, at] = (key * cosine[...] + turned * sine[...]).astype(out.dtype)
    out[:, key_width:] = (own[:, key_width:] + other[:, key_width:]).astype(out.dtype)


def finish(own, other, cosine, sine):
    tokens, features = own.shape
    tile = tokens // 3

    def block(columns):
        return pl.BlockSpec((tile, columns), lambda i: (i, 0))

    return pl.pallas_call(
        finish_kernel,
        out_shape=jax.ShapeDtypeStruct((tokens, features), jnp.bfloat16),
        grid=(3,),
        in_specs=[block(features), block(features), block(HEAD), block(HEAD)],
        out_specs=block(features),
        name="finish",
    )(own, other, cosine, sine)


ENTRY = 5
ARRIVALS = ((0, 0), (0, 1), (-1, 0), (1, 0), (-1, 1), (1, 1), (2, 0), (2, 1))


def plan_kernel(xs, zs, table, place, out, lows, highs):
    x_at, z_at = place[0], place[1]
    mine = table[2 * (x_at * zs + z_at)]
    for call in range(2):
        skip = 1 - call
        shards_in = ARRIVALS[4 * call : 4 * call + 4]
        others = 4 - skip
        low_count = jnp.int32(0)
        high_count = jnp.int32(others)
        for slot in range(skip, 4):
            dx, dz = shards_in[slot]
            low = table[2 * ((x_at + dx + xs) % xs * zs + (z_at + dz) % zs)]
            under = jnp.where(low < mine, 1, 0)
            highs[slot - skip] = 2 * slot
            lows[low_count] = 2 * slot
            highs[high_count] = 2 * slot + 1
            low_count = low_count + under
            high_count = high_count + 1 - under
        begin = call * STEPS * ENTRY
        shift = 0
        if skip:
            fixed = (0, 0, lows[0], 0, jnp.where(low_count == 0, 1, 0), 1, 1, 0, 0, 0)
            for i, value in enumerate(fixed):
                out[begin + i] = jnp.int32(value)
            shift = 1
            low_count = jnp.maximum(low_count - 1, 0)
        low_full, high_full = low_count // 2, high_count // 2
        low_odd, high_odd = low_count % 2, high_count % 2
        for step in range(STEPS - 2 * skip):
            after = step - low_full - high_full
            in_low = step < low_full
            full = after < 0
            end_low = (after == 0) & (low_odd == 1)
            end_high = (after == low_odd) & (high_odd == 1)
            is_low = in_low | end_low
            at_low = jnp.where(in_low, 2 * step, jnp.maximum(low_count - 1, 0))
            at_high = jnp.where(full, jnp.maximum(2 * (step - low_full), 0), high_count - 1)
            key_a = jnp.where(is_low, lows[shift + at_low], highs[at_high])
            key_a = jnp.where(full | end_low | end_high, key_a, 0)
            key_b = jnp.where(is_low, lows[shift + at_low + 1], highs[at_high + 1])
            key_b = jnp.where(full, key_b, key_a)
            entry = begin + (2 * skip + step) * ENTRY
            out[entry] = jnp.where(is_low, 0, 1)
            out[entry + 1] = key_a
            out[entry + 2] = key_b
            out[entry + 3] = jnp.where(full | end_low | end_high, 0, 1)
            out[entry + 4] = jnp.where(full, 0, 1)


def plan(table, place):
    xs, zs = lax.axis_size("x"), lax.axis_size("zl")

    def body(*refs):
        plan_kernel(xs, zs, *refs)

    in_smem = pl.BlockSpec(memory_space=pltpu.SMEM)
    return pl.pallas_call(
        body,
        out_shape=jax.ShapeDtypeStruct((2 * STEPS * ENTRY,), jnp.int32),
        in_specs=[in_smem, in_smem],
        out_specs=in_smem,
        scratch_shapes=[pltpu.SMEM((16,), jnp.int32), pltpu.SMEM((16,), jnp.int32)],
        name="plan",
    )(table, place)


def attend_kernel(moves, first, last, steps, queries, *refs):
    sources = len(moves)
    keys, values = refs[:sources], refs[sources : 2 * sources]
    rest = list(refs[2 * sources :])
    if not first:
        carried, packed_in = rest.pop(0), rest.pop(0)
    if last:
        out = rest.pop(0)
    else:
        kept, packed_out = rest.pop(0), rest.pop(0)
    if last:
        packed, key_rows, value_rows, corner, best, sums = rest
    else:
        packed, key_rows, value_rows, corner = rest
        best, sums = packed_out.at[0], kept.at[0]
    half = queries.shape[0] // 2
    stack = GROUPS * half
    scale = math.log2(math.e) / math.sqrt(HEAD)
    span = SPAN
    chunks = stack // span

    if first:

        @pl.when(pl.program_id(0) == 0)
        def _():
            lane = lax.broadcasted_iota(jnp.int32, corner.shape, 1)
            row = lax.broadcasted_iota(jnp.int32, corner.shape, 0)
            corner[...] = jnp.where(row <= lax.rem(lane, half), 0.0, LOW)

    for source, pieces in enumerate(moves):
        for start, segment, place, size in pieces:
            key_rows[segment, place : place + size] = keys[source][start : start + size]
            value_rows[segment, place : place + size] = values[source][start : start + size]
    for part in range(2):
        for group in range(GROUPS):
            packed[part, group * half : (group + 1) * half, :] = queries[
                part * half : (part + 1) * half, group * HEAD : (group + 1) * HEAD
            ]
    if not first:
        best[...] = packed_in[0]
        sums[...] = carried[0]

    seen = []
    for step in range(STEPS):
        entry = (step if first else STEPS + step) * ENTRY
        fresh = first and step < 2
        part = step if fresh else steps[entry]
        key_a, key_b = steps[entry + 1], steps[entry + 2]
        key = jnp.concatenate([key_rows[key_a], key_rows[key_b]], axis=0)
        value = jnp.concatenate([value_rows[key_a], value_rows[key_b]], axis=0)
        turned = jnp.concatenate([value.T, jnp.ones((16, 2 * half), value.dtype)], axis=0)
        seen.append((entry, fresh, part, key, turned))

    def raw(unit):
        _, _, part, key, _ = seen[unit // chunks]
        at = unit % chunks * span
        return lax.dot_general(
            key, packed[part, at : at + span, :], (((1,), (1,)), ((), ())), preferred_element_type=jnp.float32
        )

    units = STEPS * chunks
    scores = [raw(unit) for unit in range(AHEAD)]
    for unit in range(units):
        step = unit // chunks
        entry, fresh, part, key, turned = seen[step]
        at = slice(unit % chunks * span, (unit % chunks + 1) * span)
        score = scores[unit]
        scores[unit] = None
        upper, lower = score[:half], score[half:]
        if fresh:
            upper = upper + corner[:, at]
        if not first and step == STEPS - 1:
            upper = upper + jnp.where(steps[entry + 3] == 1, LOW, 0.0)
        if (first and step in (0, STEPS - 1)) or (not first and step >= STEPS - 2):
            lower = lower + jnp.where(steps[entry + 4] == 1, LOW, 0.0)
        score = jnp.concatenate([upper, lower], axis=0)
        new = jnp.max(score, axis=0, keepdims=True)
        if not fresh:
            old = best[part, :, at]
            new = jnp.maximum(old, new)
        best[part, :, at] = new
        weight = jnp.exp2((score - new) * scale).astype(jnp.bfloat16)
        if unit + AHEAD < units:
            scores.append(raw(unit + AHEAD))
        more = jnp.dot(turned, weight, preferred_element_type=jnp.float32)[: HEAD + 8]
        if not fresh:
            more = sums[part, :, at] * jnp.exp2((old - new) * scale) + more
        sums[part, :, at] = more

    if not last:
        return
    for part in range(2):
        share = 1.0 / sums[part, HEAD : HEAD + 1, :]
        for group in range(0, GROUPS, 2):
            at = slice(group * half, (group + 2) * half)
            done = (sums[part, :HEAD, at] * share[:, at]).T.astype(out.dtype)
            for side in range(2):
                out[
                    part * half : (part + 1) * half, (group + side) * HEAD : (group + side + 1) * HEAD
                ] = done[side * half : (side + 1) * half]


def attend(queries, arrays, moves, steps, carried=None, last=True):
    tokens, width = queries.shape
    half = tokens // 2
    stack = GROUPS * half
    segments = 1 + max(piece[1] for pieces in moves for piece in pieces)
    first = carried is None

    def body(*refs):
        attend_kernel(moves, first, last, *refs)

    def column(offset):
        return [
            pl.BlockSpec((a.shape[0], HEAD), lambda h, s, offset=offset: (0, offset + h)) for a in arrays
        ]

    state_specs = [
        pl.BlockSpec((1, 2, HEAD + 8, stack), lambda h, s: (h, 0, 0, 0)),
        pl.BlockSpec((1, 2, 1, stack), lambda h, s: (h, 0, 0, 0)),
    ]
    wide = pl.BlockSpec((tokens, GROUPS * HEAD), lambda h, s: (0, h))
    if last:
        out_shape = jax.ShapeDtypeStruct((tokens, width), jnp.bfloat16)
        out_specs = wide
    else:
        out_shape = [
            pltpu.HBM((KV_HEADS, 2, HEAD + 8, stack), jnp.float32),
            pltpu.HBM((KV_HEADS, 2, 1, stack), jnp.float32),
        ]
        out_specs = state_specs
    if not first:
        carried = [pltpu.with_memory_space_constraint(a, pltpu.HBM) for a in carried]
    queries = pltpu.with_memory_space_constraint(queries, pltpu.HBM)
    return pl.pallas_call(
        body,
        out_shape=out_shape,
        grid_spec=pltpu.PrefetchScalarGridSpec(
            num_scalar_prefetch=1,
            grid=(KV_HEADS,),
            in_specs=[wide] + column(0) + column(KV_HEADS) + ([] if first else state_specs),
            out_specs=out_specs,
            scratch_shapes=[
                pltpu.VMEM((2, stack, HEAD), jnp.bfloat16),
                pltpu.VMEM((segments, half, HEAD), jnp.bfloat16),
                pltpu.VMEM((segments, half, HEAD), jnp.bfloat16),
                pltpu.VMEM((half, stack), jnp.float32),
            ]
            + (
                [
                    pltpu.VMEM((2, 1, stack), jnp.float32),
                    pltpu.VMEM((2, HEAD + 8, stack), jnp.float32),
                ]
                if last
                else []
            ),
        ),
        compiler_params=pltpu.CompilerParams(vmem_limit_bytes=40 << 20),
        cost_estimate=pl.CostEstimate(
            flops=2 * 2 * Q_HEADS * (segments + 1) * half * half * HEAD * 2,
            transcendentals=Q_HEADS * (segments + 1) * half * half,
            bytes_accessed=30 << 20,
        ),
        name="attend_last" if last else "attend_first",
    )(steps, queries, *arrays, *arrays, *(() if first else carried))


SPAN = 256
STEPS = 5
AHEAD = 8


def shards(
    hidden, queries, weights_old, gradient_old, first_old, second_old, old_owner, new_owner, offsets
):
    devices = old_owner.shape[0]
    tok_rows = hidden.shape[1]
    half_tok = tok_rows // 2
    updated = adam_step(weights_old, gradient_old, first_old, second_old)
    copies = updated[0].astype(jnp.bfloat16)
    split = [copies[:, first:last] for first, last in PARTS]
    planes = [around(around(p, o[0]), o[1]) for p, o in zip(split, ORDERS, strict=True)]

    x_at, zl_at, y_at = lax.axis_index("x"), lax.axis_index("zl"), lax.axis_index("y")
    z_at, core = lax.axis_index(DEPTH), lax.axis_index("c")
    xs, ys, zs = lax.axis_size("x"), lax.axis_size("y"), lax.axis_size(DEPTH)
    pair = lax.axis_size("zl")
    table = offsets[0]
    mine = table[x_at * pair + zl_at]
    local = jnp.arange(tok_rows, dtype=jnp.int32)
    query_pos = jnp.where(local < half_tok, mine[0] + local, mine[1] + local - half_tok)
    exponent = jnp.arange(HEAD // 2, dtype=jnp.float32) * (2.0 / HEAD)
    inv_freq = jnp.power(rope_base, -exponent)
    angles = query_pos.astype(jnp.float32)[:, None] * inv_freq
    cosine, sine = jnp.cos(angles), jnp.sin(angles)
    cosine = jnp.concatenate([cosine, cosine], axis=1)
    sine = jnp.concatenate([-sine, sine], axis=1)
    steps = plan(table.reshape(-1), jnp.stack([x_at, zl_at]).astype(jnp.int32))

    spot = jnp.arange(devices, dtype=jnp.int32)
    side = len(OFFSETS)
    which = spot // (devices // 2)
    iz, ix, iy = spot // side**2 % side, spot // side % side, spot % side

    def shifted(index):
        return jnp.where(index == 1, -1, jnp.where(index > 1, index - 1, 0))

    at_z = (z_at + shifted(iz) + zs) % zs
    at_x = (x_at + shifted(ix) + xs) % xs
    at_y = (y_at + shifted(iy) + ys) % ys
    at_core = jnp.where(which == 0, core, 1 - core)
    device = ((at_z // pair * ys + at_y) * 2 + at_core) * (xs * pair) + at_x * pair + at_z % pair
    blocks = jnp.take(old_owner, device, axis=0)

    blocks, planes, cosine, sine, steps = lax.optimization_barrier(
        (blocks, planes, cosine, sine, steps)
    )
    chosen = choose_columns(hidden[0], blocks)
    swap = [(0, 1), (1, 0)]
    others = lax.ppermute(chosen[1], "c", swap)
    arrays = []
    for plane, axes in zip(planes, ORDERS, strict=True):
        arrays += around_last(plane, axes[2])
    theirs, ours = partial_products(others, chosen[0], arrays)
    received = lax.ppermute(theirs, "c", swap)
    rows_own = finish(ours, received, cosine, sine)
    moved = relocate(jnp.stack(updated), new_owner, old_owner)
    weights_new, first_new, second_new = (moved[0], moved[1], moved[2])
    near = [(i, i ^ 1) for i in range(pair)]
    ahead = [(i, (i + 1) % xs) for i in range(xs)]
    behind = [(i, (i - 1) % xs) for i in range(xs)]
    z_rows = lax.ppermute(rows_own, "zl", near)
    left = lax.ppermute(rows_own, "x", ahead)
    right = lax.ppermute(rows_own, "x", behind)
    left_z = lax.ppermute(left, "zl", near)
    right_z = lax.ppermute(z_rows, "x", behind)
    far = lax.ppermute(left, "x", ahead)
    halves = [(0, 0, half_tok), (half_tok, 1, half_tok)]
    moves = [[(start, 2 * i + seg, 0, size) for start, seg, size in halves] for i in range(4)]
    state = attend(queries[0], [rows_own, z_rows, left, right], moves, steps, last=False)
    left_z, right_z, far, state = lax.optimization_barrier((left_z, right_z, far, state))
    third = tok_rows // 3
    last_z = lax.ppermute(far[:third], "zl", near)
    last_left = lax.ppermute(left_z[third : 2 * third], "x", ahead)
    last_right = lax.ppermute(right_z[2 * third :], "x", behind)
    moves = moves[:3] + [
        [(0, 6, 0, third)],
        [(0, 6, third, half_tok - third), (half_tok - third, 7, 0, 2 * third - half_tok)],
        [(0, 7, 2 * third - half_tok, third)],
    ]
    attended = attend(
        queries[0], [left_z, right_z, far, last_z, last_left, last_right], moves, steps, carried=state
    )
    return (weights_new, first_new, second_new, attended[None])


def solution(mesh):
    grid = Mesh(mesh.devices.reshape(2, 4, 2, 4, 2), ALL)
    in_specs = (
        P(DP, CTX, None),
        P(DP, CTX, None),
        P(ALL, None),
        P(ALL, None),
        P(ALL, None),
        P(ALL, None),
        P(),
        P(),
        P(DP, None, None),
    )
    out_specs = (
        P(ALL, None),
        P(ALL, None),
        P(ALL, None),
        P(DP, CTX, None),
    )
    return jax.shard_map(shards, mesh=grid, in_specs=in_specs, out_specs=out_specs, check_vma=False)
```

```python
import math

import jax
import jax.numpy as jnp
from jax import lax
from jax.experimental import pallas as pl
from jax.experimental.pallas import tpu as pltpu
from jax.sharding import Mesh
from jax.sharding import PartitionSpec as P

HEAD = 128
KV_HEADS = 4
Q_HEADS = 32
GROUPS = Q_HEADS // KV_HEADS
DP = ("zh", "y", "c")
CTX = ("x", "zl")
ALL = DP + CTX
TORUS = ("zh", "zl", "x", "y", "c")
LOW = -1e30


learn_rate = 0.0003
beta_one = 0.9
beta_two = 0.95
adam_eps = 1e-08
decay_rate = 0.1
step_number = 1000
corr_one = 1.0 - beta_one**step_number
corr_two = 1.0 - beta_two**step_number
rope_base = 500000.0


def in_blocks(value, dim, peers):
    before, after = (value.shape[:dim], value.shape[dim + 1 :])
    return jnp.moveaxis(value.reshape(*before, peers, -1, *after), dim, 0)


def adam_step(weights, gradient, first_mom, second_mom):
    first_next = beta_one * first_mom + (1.0 - beta_one) * gradient
    second_next = beta_two * second_mom + (1.0 - beta_two) * gradient * gradient
    direction = first_next / corr_one / (jnp.sqrt(second_next / corr_two) + adam_eps)
    weights_next = weights - learn_rate * (direction + decay_rate * weights)
    return (weights_next, first_next, second_next)


def invert(owners):
    devices = owners.shape[0]
    return jnp.zeros((devices,), jnp.int32).at[owners].set(jnp.arange(devices, dtype=jnp.int32))


def relocate(stacked, new_owner, old_owner):
    states_count, row_count, proj_width = stacked.shape
    devices = new_owner.shape[0]
    col_count = proj_width // devices
    outgoing = stacked.reshape(states_count, row_count, devices, col_count).transpose(2, 0, 3, 1)
    outgoing = jnp.take(outgoing, new_owner, axis=0)
    incoming = lax.all_to_all(outgoing, ALL, split_axis=0, concat_axis=0, tiled=True)
    ordered = jnp.take(incoming, invert(old_owner), axis=0)
    return ordered.transpose(1, 2, 0, 3).reshape(states_count, col_count, devices * row_count)


def project_kernel(source, hidden, gathered, cosine, sine, out, rows, cols, sums, row_sem, col_sem):
    blocks, block_rows, _ = gathered.shape
    tokens, width = hidden.shape
    chunks = row_sem.shape[0]
    per = blocks // chunks
    span = width // chunks

    def row_copy(block, chunk):
        return pltpu.make_async_copy(
            gathered.at[source[block]],
            rows.at[pl.ds(pl.multiple_of(block * block_rows, block_rows), block_rows)],
            row_sem.at[chunk],
        )

    def col_copy(chunk):
        return pltpu.make_async_copy(
            hidden.at[:, pl.ds(chunk * span, span)],
            cols.at[:, pl.ds(chunk * span, span)],
            col_sem.at[chunk],
        )

    for chunk in range(chunks):
        col_copy(chunk).start()

        def issue(i, carry, chunk=chunk):
            row_copy(chunk * per + i, chunk).start()
            return carry

        lax.fori_loop(0, per, issue, 0)
    for chunk in range(chunks):
        col_copy(chunk).wait()
        whole = rows.at[pl.ds(chunk * span, span)]
        pltpu.make_async_copy(whole, whole, row_sem.at[chunk]).wait()
        part = jnp.dot(
            cols[:, chunk * span : (chunk + 1) * span],
            rows[chunk * span : (chunk + 1) * span, :],
            preferred_element_type=jnp.float32,
        )
        if chunk == 0:
            sums[...] = part
        else:
            sums[...] += part
    for head in range(KV_HEADS):
        key = sums[:, head * HEAD : (head + 1) * HEAD]
        turned = pltpu.roll(key, HEAD // 2, 1)
        out[:, head * HEAD : (head + 1) * HEAD] = (
            key * cosine[...] + turned * sine[...]
        ).astype(out.dtype)
    key_width = KV_HEADS * HEAD
    out[:, key_width:] = sums[:, key_width:].astype(out.dtype)


def project(hidden, gathered, source, cosine, sine):
    tokens, width = hidden.shape
    blocks, block_rows, features = gathered.shape
    chunks = 8
    return pl.pallas_call(
        project_kernel,
        out_shape=jax.ShapeDtypeStruct((tokens, features), jnp.bfloat16),
        grid_spec=pltpu.PrefetchScalarGridSpec(
            num_scalar_prefetch=1,
            grid=(1,),
            in_specs=[
                pl.BlockSpec(memory_space=pltpu.HBM),
                pl.BlockSpec(memory_space=pltpu.HBM),
                pl.BlockSpec((tokens, HEAD), lambda i, s: (0, 0)),
                pl.BlockSpec((tokens, HEAD), lambda i, s: (0, 0)),
            ],
            out_specs=pl.BlockSpec((tokens, features), lambda i, s: (0, 0)),
            scratch_shapes=[
                pltpu.VMEM((width, features), jnp.bfloat16),
                pltpu.VMEM((tokens, width), jnp.bfloat16),
                pltpu.VMEM((tokens, features), jnp.float32),
                pltpu.SemaphoreType.DMA((chunks,)),
                pltpu.SemaphoreType.DMA((chunks,)),
            ],
        ),
        compiler_params=pltpu.CompilerParams(vmem_limit_bytes=44 << 20),
        name="project",
    )(source, hidden, gathered, cosine, sine)


ENTRY = 5
ARRIVALS = ((0, 0), (0, 1), (-1, 0), (1, 0), (-1, 1), (1, 1), (2, 0), (2, 1))


def plan_kernel(xs, zs, table, place, out, lows, highs):
    x_at, z_at = place[0], place[1]
    mine = table[2 * (x_at * zs + z_at)]
    for call in range(2):
        skip = 1 - call
        shards_in = ARRIVALS[4 * call : 4 * call + 4]
        others = 4 - skip
        low_count = jnp.int32(0)
        high_count = jnp.int32(others)
        for slot in range(skip, 4):
            dx, dz = shards_in[slot]
            low = table[2 * ((x_at + dx + xs) % xs * zs + (z_at + dz) % zs)]
            under = jnp.where(low < mine, 1, 0)
            highs[slot - skip] = 2 * slot
            lows[low_count] = 2 * slot
            highs[high_count] = 2 * slot + 1
            low_count = low_count + under
            high_count = high_count + 1 - under
        begin = call * STEPS * ENTRY
        shift = 0
        if skip:
            fixed = (0, 0, lows[0], 0, jnp.where(low_count == 0, 1, 0), 1, 1, 0, 0, 0)
            for i, value in enumerate(fixed):
                out[begin + i] = jnp.int32(value)
            shift = 1
            low_count = jnp.maximum(low_count - 1, 0)
        low_full, high_full = low_count // 2, high_count // 2
        low_odd, high_odd = low_count % 2, high_count % 2
        for step in range(STEPS - 2 * skip):
            after = step - low_full - high_full
            in_low = step < low_full
            full = after < 0
            end_low = (after == 0) & (low_odd == 1)
            end_high = (after == low_odd) & (high_odd == 1)
            is_low = in_low | end_low
            at_low = jnp.where(in_low, 2 * step, jnp.maximum(low_count - 1, 0))
            at_high = jnp.where(full, jnp.maximum(2 * (step - low_full), 0), high_count - 1)
            key_a = jnp.where(is_low, lows[shift + at_low], highs[at_high])
            key_a = jnp.where(full | end_low | end_high, key_a, 0)
            key_b = jnp.where(is_low, lows[shift + at_low + 1], highs[at_high + 1])
            key_b = jnp.where(full, key_b, key_a)
            entry = begin + (2 * skip + step) * ENTRY
            out[entry] = jnp.where(is_low, 0, 1)
            out[entry + 1] = key_a
            out[entry + 2] = key_b
            out[entry + 3] = jnp.where(full | end_low | end_high, 0, 1)
            out[entry + 4] = jnp.where(full, 0, 1)


def plan(table, place):
    xs, zs = lax.axis_size("x"), lax.axis_size("zl")

    def body(*refs):
        plan_kernel(xs, zs, *refs)

    in_smem = pl.BlockSpec(memory_space=pltpu.SMEM)
    return pl.pallas_call(
        body,
        out_shape=jax.ShapeDtypeStruct((2 * STEPS * ENTRY,), jnp.int32),
        in_specs=[in_smem, in_smem],
        out_specs=in_smem,
        scratch_shapes=[pltpu.SMEM((16,), jnp.int32), pltpu.SMEM((16,), jnp.int32)],
        name="plan",
    )(table, place)


def attend_kernel(moves, first, last, steps, queries, *refs):
    sources = len(moves)
    keys, values = refs[:sources], refs[sources : 2 * sources]
    rest = list(refs[2 * sources :])
    if not first:
        carried, packed_in = rest.pop(0), rest.pop(0)
    if last:
        out = rest.pop(0)
    else:
        kept, packed_out = rest.pop(0), rest.pop(0)
    if last:
        packed, key_rows, value_rows, corner, best, sums = rest
    else:
        packed, key_rows, value_rows, corner = rest
        best, sums = packed_out.at[0], kept.at[0]
    half = queries.shape[0] // 2
    stack = GROUPS * half
    scale = math.log2(math.e) / math.sqrt(HEAD)
    span = SPAN
    chunks = stack // span

    if first:

        @pl.when(pl.program_id(0) == 0)
        def _():
            lane = lax.broadcasted_iota(jnp.int32, corner.shape, 1)
            row = lax.broadcasted_iota(jnp.int32, corner.shape, 0)
            corner[...] = jnp.where(row <= lax.rem(lane, half), 0.0, LOW)

    for source, pieces in enumerate(moves):
        for start, segment, place, size in pieces:
            key_rows[segment, place : place + size] = keys[source][start : start + size]
            value_rows[segment, place : place + size] = values[source][start : start + size]
    for part in range(2):
        for group in range(GROUPS):
            packed[part, group * half : (group + 1) * half, :] = queries[
                part * half : (part + 1) * half, group * HEAD : (group + 1) * HEAD
            ]
    if not first:
        best[...] = packed_in[0]
        sums[...] = carried[0]

    seen = []
    for step in range(STEPS):
        entry = (step if first else STEPS + step) * ENTRY
        fresh = first and step < 2
        part = step if fresh else steps[entry]
        key_a, key_b = steps[entry + 1], steps[entry + 2]
        key = jnp.concatenate([key_rows[key_a], key_rows[key_b]], axis=0)
        value = jnp.concatenate([value_rows[key_a], value_rows[key_b]], axis=0)
        turned = jnp.concatenate([value.T, jnp.ones((16, 2 * half), value.dtype)], axis=0)
        seen.append((entry, fresh, part, key, turned))

    def raw(unit):
        _, _, part, key, _ = seen[unit // chunks]
        at = unit % chunks * span
        return lax.dot_general(
            key, packed[part, at : at + span, :], (((1,), (1,)), ((), ())), preferred_element_type=jnp.float32
        )

    units = STEPS * chunks
    scores = [raw(unit) for unit in range(AHEAD)]
    for unit in range(units):
        step = unit // chunks
        entry, fresh, part, key, turned = seen[step]
        at = slice(unit % chunks * span, (unit % chunks + 1) * span)
        score = scores[unit]
        scores[unit] = None
        upper, lower = score[:half], score[half:]
        if fresh:
            upper = upper + corner[:, at]
        if not first and step == STEPS - 1:
            upper = upper + jnp.where(steps[entry + 3] == 1, LOW, 0.0)
        if (first and step in (0, STEPS - 1)) or (not first and step >= STEPS - 2):
            lower = lower + jnp.where(steps[entry + 4] == 1, LOW, 0.0)
        score = jnp.concatenate([upper, lower], axis=0)
        new = jnp.max(score, axis=0, keepdims=True)
        if not fresh:
            old = best[part, :, at]
            new = jnp.maximum(old, new)
        best[part, :, at] = new
        weight = jnp.exp2((score - new) * scale).astype(jnp.bfloat16)
        if unit + AHEAD < units:
            scores.append(raw(unit + AHEAD))
        more = jnp.dot(turned, weight, preferred_element_type=jnp.float32)[: HEAD + 8]
        if not fresh:
            more = sums[part, :, at] * jnp.exp2((old - new) * scale) + more
        sums[part, :, at] = more

    if not last:
        return
    for part in range(2):
        share = 1.0 / sums[part, HEAD : HEAD + 1, :]
        for group in range(0, GROUPS, 2):
            at = slice(group * half, (group + 2) * half)
            done = (sums[part, :HEAD, at] * share[:, at]).T.astype(out.dtype)
            for side in range(2):
                out[
                    part * half : (part + 1) * half, (group + side) * HEAD : (group + side + 1) * HEAD
                ] = done[side * half : (side + 1) * half]


def attend(queries, arrays, moves, steps, carried=None, last=True):
    tokens, width = queries.shape
    half = tokens // 2
    stack = GROUPS * half
    segments = 1 + max(piece[1] for pieces in moves for piece in pieces)
    first = carried is None

    def body(*refs):
        attend_kernel(moves, first, last, *refs)

    def column(offset):
        return [
            pl.BlockSpec((a.shape[0], HEAD), lambda h, s, offset=offset: (0, offset + h)) for a in arrays
        ]

    state_specs = [
        pl.BlockSpec((1, 2, HEAD + 8, stack), lambda h, s: (h, 0, 0, 0)),
        pl.BlockSpec((1, 2, 1, stack), lambda h, s: (h, 0, 0, 0)),
    ]
    wide = pl.BlockSpec((tokens, GROUPS * HEAD), lambda h, s: (0, h))
    if last:
        out_shape = jax.ShapeDtypeStruct((tokens, width), jnp.bfloat16)
        out_specs = wide
    else:
        out_shape = [
            pltpu.HBM((KV_HEADS, 2, HEAD + 8, stack), jnp.float32),
            pltpu.HBM((KV_HEADS, 2, 1, stack), jnp.float32),
        ]
        out_specs = state_specs
    if not first:
        carried = [pltpu.with_memory_space_constraint(a, pltpu.HBM) for a in carried]
    queries = pltpu.with_memory_space_constraint(queries, pltpu.HBM)
    return pl.pallas_call(
        body,
        out_shape=out_shape,
        grid_spec=pltpu.PrefetchScalarGridSpec(
            num_scalar_prefetch=1,
            grid=(KV_HEADS,),
            in_specs=[wide] + column(0) + column(KV_HEADS) + ([] if first else state_specs),
            out_specs=out_specs,
            scratch_shapes=[
                pltpu.VMEM((2, stack, HEAD), jnp.bfloat16),
                pltpu.VMEM((segments, half, HEAD), jnp.bfloat16),
                pltpu.VMEM((segments, half, HEAD), jnp.bfloat16),
                pltpu.VMEM((half, stack), jnp.float32),
            ]
            + (
                [
                    pltpu.VMEM((2, 1, stack), jnp.float32),
                    pltpu.VMEM((2, HEAD + 8, stack), jnp.float32),
                ]
                if last
                else []
            ),
        ),
        compiler_params=pltpu.CompilerParams(vmem_limit_bytes=40 << 20, flags=FLAGS),
        cost_estimate=pl.CostEstimate(
            flops=2 * 2 * Q_HEADS * (segments + 1) * half * half * HEAD * 2,
            transcendentals=Q_HEADS * (segments + 1) * half * half,
            bytes_accessed=30 << 20,
        ),
        name="attend_last" if last else "attend_first",
    )(steps, queries, *arrays, *arrays, *(() if first else carried))


SPAN = 256
STEPS = 5
AHEAD = 8
FLAGS = {}


def shards(
    hidden, queries, weights_old, gradient_old, first_old, second_old, old_owner, new_owner, offsets
):
    devices = old_owner.shape[0]
    row_count, proj_width = weights_old.shape
    tok_rows = hidden.shape[1]
    half_tok = tok_rows // 2
    sizes = [lax.axis_size(a) for a in ALL]
    copies = adam_step(weights_old, gradient_old, first_old, second_old)[0].astype(jnp.bfloat16)
    gathered = lax.all_gather(copies, TORUS, axis=0, tiled=False).reshape(
        devices, row_count, proj_width
    )
    owner_at = old_owner.reshape(sizes).transpose([ALL.index(a) for a in TORUS]).reshape(devices)
    source = invert(owner_at)
    states = lax.optimization_barrier((weights_old, gradient_old, first_old, second_old, copies))[:4]
    moved = relocate(jnp.stack(adam_step(*states)), new_owner, old_owner)

    x_at, zl_at = lax.axis_index("x"), lax.axis_index("zl")
    pair = lax.axis_size("zl")
    table = offsets[0]
    mine = table[x_at * pair + zl_at]
    local = jnp.arange(tok_rows, dtype=jnp.int32)
    query_pos = jnp.where(local < half_tok, mine[0] + local, mine[1] + local - half_tok)
    exponent = jnp.arange(HEAD // 2, dtype=jnp.float32) * (2.0 / HEAD)
    inv_freq = jnp.power(rope_base, -exponent)
    angles = query_pos.astype(jnp.float32)[:, None] * inv_freq
    cosine, sine = jnp.cos(angles), jnp.sin(angles)
    cosine = jnp.concatenate([cosine, cosine], axis=1)
    sine = jnp.concatenate([-sine, sine], axis=1)

    xs = lax.axis_size("x")
    steps = plan(table.reshape(-1), jnp.stack([x_at, zl_at]).astype(jnp.int32))

    gathered, source, cosine, sine, steps, moved = lax.optimization_barrier(
        (gathered, source, cosine, sine, steps, moved)
    )
    weights_new, first_new, second_new = (moved[0], moved[1], moved[2])
    in_hbm = pltpu.with_memory_space_constraint(hidden[0], pltpu.HBM)
    rows_own = project(in_hbm, gathered, source, cosine, sine)
    near = [(i, i ^ 1) for i in range(pair)]
    ahead = [(i, (i + 1) % xs) for i in range(xs)]
    behind = [(i, (i - 1) % xs) for i in range(xs)]
    z_rows = lax.ppermute(rows_own, "zl", near)
    left = lax.ppermute(rows_own, "x", ahead)
    right = lax.ppermute(rows_own, "x", behind)
    left_z = lax.ppermute(left, "zl", near)
    right_z = lax.ppermute(z_rows, "x", behind)
    far = lax.ppermute(left, "x", ahead)
    halves = [(0, 0, half_tok), (half_tok, 1, half_tok)]
    moves = [[(start, 2 * i + seg, 0, size) for start, seg, size in halves] for i in range(4)]
    state = attend(queries[0], [rows_own, z_rows, left, right], moves, steps, last=False)
    left_z, right_z, far, state = lax.optimization_barrier((left_z, right_z, far, state))
    third = tok_rows // 3
    last_z = lax.ppermute(far[:third], "zl", near)
    last_left = lax.ppermute(left_z[third : 2 * third], "x", ahead)
    last_right = lax.ppermute(right_z[2 * third :], "x", behind)
    moves = moves[:3] + [
        [(0, 6, 0, third)],
        [(0, 6, third, half_tok - third), (half_tok - third, 7, 0, 2 * third - half_tok)],
        [(0, 7, 2 * third - half_tok, third)],
    ]
    attended = attend(
        queries[0], [left_z, right_z, far, last_z, last_left, last_right], moves, steps, carried=state
    )
    return (weights_new, first_new, second_new, attended[None])


def solution(mesh):
    grid = Mesh(mesh.devices.reshape(2, 4, 2, 4, 2), ALL)
    in_specs = (
        P(DP, CTX, None),
        P(DP, CTX, None),
        P(ALL, None),
        P(ALL, None),
        P(ALL, None),
        P(ALL, None),
        P(),
        P(),
        P(DP, None, None),
    )
    out_specs = (
        P(ALL, None),
        P(ALL, None),
        P(ALL, None),
        P(DP, CTX, None),
    )
    return jax.shard_map(shards, mesh=grid, in_specs=in_specs, out_specs=out_specs, check_vma=False)
```

```python
import math

import jax
import jax.numpy as jnp
from jax import lax
from jax.experimental import pallas as pl
from jax.experimental.pallas import tpu as pltpu
from jax.sharding import Mesh
from jax.sharding import PartitionSpec as P

HEAD = 128
KV_HEADS = 4
Q_HEADS = 32
GROUPS = Q_HEADS // KV_HEADS
DP = ("zh", "y", "c")
CTX = ("x", "zl")
ALL = DP + CTX
TORUS = ("zh", "zl", "x", "y", "c")
LOW = -1e30


learn_rate = 0.0003
beta_one = 0.9
beta_two = 0.95
adam_eps = 1e-08
decay_rate = 0.1
step_number = 1000
corr_one = 1.0 - beta_one**step_number
corr_two = 1.0 - beta_two**step_number
rope_base = 500000.0


def in_blocks(value, dim, peers):
    before, after = (value.shape[:dim], value.shape[dim + 1 :])
    return jnp.moveaxis(value.reshape(*before, peers, -1, *after), dim, 0)


def adam_step(weights, gradient, first_mom, second_mom):
    first_next = beta_one * first_mom + (1.0 - beta_one) * gradient
    second_next = beta_two * second_mom + (1.0 - beta_two) * gradient * gradient
    direction = first_next / corr_one / (jnp.sqrt(second_next / corr_two) + adam_eps)
    weights_next = weights - learn_rate * (direction + decay_rate * weights)
    return (weights_next, first_next, second_next)


def invert(owners):
    devices = owners.shape[0]
    return jnp.zeros((devices,), jnp.int32).at[owners].set(jnp.arange(devices, dtype=jnp.int32))


def relocate(stacked, new_owner, old_owner):
    states_count, row_count, proj_width = stacked.shape
    devices = new_owner.shape[0]
    col_count = proj_width // devices
    outgoing = stacked.reshape(states_count, row_count, devices, col_count).transpose(2, 0, 3, 1)
    outgoing = jnp.take(outgoing, new_owner, axis=0)
    incoming = lax.all_to_all(outgoing, ALL, split_axis=0, concat_axis=0, tiled=True)
    ordered = jnp.take(incoming, invert(old_owner), axis=0)
    return ordered.transpose(1, 2, 0, 3).reshape(states_count, col_count, devices * row_count)


def project_kernel(source, hidden, gathered, cosine, sine, out, rows, cols, sums, row_sem, col_sem):
    blocks, block_rows, _ = gathered.shape
    tokens, width = hidden.shape
    chunks = row_sem.shape[0]
    per = blocks // chunks
    span = width // chunks

    def row_copy(block, chunk):
        return pltpu.make_async_copy(
            gathered.at[source[block]],
            rows.at[pl.ds(pl.multiple_of(block * block_rows, block_rows), block_rows)],
            row_sem.at[chunk],
        )

    def col_copy(chunk):
        return pltpu.make_async_copy(
            hidden.at[:, pl.ds(chunk * span, span)],
            cols.at[:, pl.ds(chunk * span, span)],
            col_sem.at[chunk],
        )

    for chunk in range(chunks):
        col_copy(chunk).start()

        def issue(i, carry, chunk=chunk):
            row_copy(chunk * per + i, chunk).start()
            return carry

        lax.fori_loop(0, per, issue, 0)
    for chunk in range(chunks):
        col_copy(chunk).wait()
        whole = rows.at[pl.ds(chunk * span, span)]
        pltpu.make_async_copy(whole, whole, row_sem.at[chunk]).wait()
        part = jnp.dot(
            cols[:, chunk * span : (chunk + 1) * span],
            rows[chunk * span : (chunk + 1) * span, :],
            preferred_element_type=jnp.float32,
        )
        if chunk == 0:
            sums[...] = part
        else:
            sums[...] += part
    for head in range(KV_HEADS):
        key = sums[:, head * HEAD : (head + 1) * HEAD]
        turned = pltpu.roll(key, HEAD // 2, 1)
        out[:, head * HEAD : (head + 1) * HEAD] = (
            key * cosine[...] + turned * sine[...]
        ).astype(out.dtype)
    key_width = KV_HEADS * HEAD
    out[:, key_width:] = sums[:, key_width:].astype(out.dtype)


def project(hidden, gathered, source, cosine, sine):
    tokens, width = hidden.shape
    blocks, block_rows, features = gathered.shape
    chunks = 8
    return pl.pallas_call(
        project_kernel,
        out_shape=jax.ShapeDtypeStruct((tokens, features), jnp.bfloat16),
        grid_spec=pltpu.PrefetchScalarGridSpec(
            num_scalar_prefetch=1,
            grid=(1,),
            in_specs=[
                pl.BlockSpec(memory_space=pltpu.HBM),
                pl.BlockSpec(memory_space=pltpu.HBM),
                pl.BlockSpec((tokens, HEAD), lambda i, s: (0, 0)),
                pl.BlockSpec((tokens, HEAD), lambda i, s: (0, 0)),
            ],
            out_specs=pl.BlockSpec((tokens, features), lambda i, s: (0, 0)),
            scratch_shapes=[
                pltpu.VMEM((width, features), jnp.bfloat16),
                pltpu.VMEM((tokens, width), jnp.bfloat16),
                pltpu.VMEM((tokens, features), jnp.float32),
                pltpu.SemaphoreType.DMA((chunks,)),
                pltpu.SemaphoreType.DMA((chunks,)),
            ],
        ),
        compiler_params=pltpu.CompilerParams(vmem_limit_bytes=44 << 20),
        name="project",
    )(source, hidden, gathered, cosine, sine)


ENTRY = 5
ARRIVALS = ((0, 0), (0, 1), (-1, 0), (1, 0), (-1, 1), (1, 1), (2, 0), (2, 1))


def plan_kernel(xs, zs, table, place, out, lows, highs):
    x_at, z_at = place[0], place[1]
    mine = table[2 * (x_at * zs + z_at)]
    for call in range(2):
        skip = 1 - call
        shards_in = ARRIVALS[4 * call : 4 * call + 4]
        others = 4 - skip
        low_count = jnp.int32(0)
        high_count = jnp.int32(others if skip else 0)
        for slot in range(skip, 4):
            dx, dz = shards_in[slot]
            low = table[2 * ((x_at + dx + xs) % xs * zs + (z_at + dz) % zs)]
            under = jnp.where(low < mine, 1, 0)
            if skip:
                highs[slot - skip] = 2 * slot
            lows[low_count] = 2 * slot
            highs[high_count] = 2 * slot + 1
            low_count = low_count + under
            high_count = high_count + 1 - under
        begin = call * STEPS * ENTRY
        shift = 0
        if skip:
            fixed = (0, 0, lows[0], 0, jnp.where(low_count == 0, 1, 0), 1, 1, 0, 0, 0)
            for i, value in enumerate(fixed):
                out[begin + i] = jnp.int32(value)
            shift = 1
            low_count = jnp.maximum(low_count - 1, 0)
        low_full, high_full = low_count // 2, high_count // 2
        low_odd, high_odd = low_count % 2, high_count % 2
        for step in range(STEPS - 2):
            after = step - low_full - high_full
            in_low = step < low_full
            full = after < 0
            end_low = (after == 0) & (low_odd == 1)
            end_high = (after == low_odd) & (high_odd == 1)
            is_low = in_low | end_low
            at_low = jnp.where(in_low, 2 * step, jnp.maximum(low_count - 1, 0))
            at_high = jnp.where(full, jnp.maximum(2 * (step - low_full), 0), jnp.maximum(high_count - 1, 0))
            key_a = jnp.where(is_low, lows[shift + at_low], highs[at_high])
            key_a = jnp.where(full | end_low | end_high, key_a, 0)
            key_b = jnp.where(is_low, lows[shift + at_low + 1], highs[at_high + 1])
            key_b = jnp.where(full, key_b, key_a)
            entry = begin + (2 + step) * ENTRY
            out[entry] = jnp.where(is_low, 0, 1)
            out[entry + 1] = key_a
            out[entry + 2] = key_b
            out[entry + 3] = jnp.where(full | end_low | end_high, 0, 1)
            out[entry + 4] = jnp.where(full, 0, 1)


def plan(table, place):
    xs, zs = lax.axis_size("x"), lax.axis_size("zl")

    def body(*refs):
        plan_kernel(xs, zs, *refs)

    in_smem = pl.BlockSpec(memory_space=pltpu.SMEM)
    return pl.pallas_call(
        body,
        out_shape=jax.ShapeDtypeStruct((2 * STEPS * ENTRY,), jnp.int32),
        in_specs=[in_smem, in_smem],
        out_specs=in_smem,
        scratch_shapes=[pltpu.SMEM((16,), jnp.int32), pltpu.SMEM((16,), jnp.int32)],
        name="plan",
    )(table, place)


def attend_kernel(moves, first, last, steps, queries, *refs):
    sources = len(moves)
    pairs = refs[:sources]
    rest = list(refs[sources:])
    if not first:
        carried, packed_in = rest.pop(0), rest.pop(0)
    if last:
        out = rest.pop(0)
    else:
        kept, packed_out = rest.pop(0), rest.pop(0)
    if last:
        key_rows, value_rows, corner, best, sums = rest
    else:
        key_rows, value_rows, corner = rest
        best, sums = packed_out.at[0], kept.at[0]
    half = queries.shape[0] // 2
    stack = GROUPS * half
    scale = math.log2(math.e) / math.sqrt(HEAD)
    span = SPAN
    chunks = stack // span

    if first:

        @pl.when(pl.program_id(0) == 0)
        def _():
            lane = lax.broadcasted_iota(jnp.int32, corner.shape, 1)
            row = lax.broadcasted_iota(jnp.int32, corner.shape, 0)
            corner[...] = jnp.where(row <= lax.rem(lane, half), 0.0, LOW)

    key_at = pl.multiple_of(pl.program_id(0) * HEAD, HEAD)
    value_at = pl.multiple_of((KV_HEADS + pl.program_id(0)) * HEAD, HEAD)
    for source, pieces in enumerate(moves):
        for start, segment, place, size in pieces:
            rows = slice(start, start + size)
            key_rows[segment, place : place + size] = pairs[source][rows, pl.ds(key_at, HEAD)]
            value_rows[segment, place : place + size] = pairs[source][rows, pl.ds(value_at, HEAD)]
    if not first:
        best[0] = packed_in[0, 0]
        sums[0] = carried[0, 0]

    seen = []
    for step in range(STEPS):
        entry = (step if first else STEPS + step) * ENTRY
        fresh = first and step < 2
        if not first and step < 2:
            part, key_a, key_b = 1, 4 * step, 4 * step + 2
        else:
            part = step if fresh else steps[entry]
            key_a, key_b = steps[entry + 1], steps[entry + 2]
        key = jnp.concatenate([key_rows[key_a], key_rows[key_b]], axis=0)
        value = jnp.concatenate([value_rows[key_a], value_rows[key_b]], axis=0)
        turned = jnp.concatenate([value.T, jnp.ones((16, 2 * half), value.dtype)], axis=0)
        seen.append((entry, fresh, part, key, turned))

    def raw(unit):
        _, _, part, key, _ = seen[unit // chunks]
        at = unit % chunks * span
        pieces = []
        while at < unit % chunks * span + span:
            group, row = at // half, at % half
            size = min(half - row, unit % chunks * span + span - at)
            rows = pl.ds(part * half + row, size)
            if not isinstance(part, int):
                rows = pl.ds(pl.multiple_of(part * half, half) + row, size)
            pieces.append(queries[rows, group * HEAD : (group + 1) * HEAD])
            at += size
        return lax.dot_general(
            key, jnp.concatenate(pieces, axis=0), (((1,), (1,)), ((), ())), preferred_element_type=jnp.float32
        )

    units = STEPS * chunks
    scores = [raw(unit) for unit in range(AHEAD)]
    for unit in range(units):
        step = unit // chunks
        entry, fresh, part, key, turned = seen[step]
        at = slice(unit % chunks * span, (unit % chunks + 1) * span)
        score = scores[unit]
        scores[unit] = None
        upper, lower = score[:half], score[half:]
        if fresh:
            upper = upper + corner[:, at]
        if not first and step == STEPS - 1:
            upper = upper + jnp.where(steps[entry + 3] == 1, LOW, 0.0)
        if (first and step in (0, STEPS - 1)) or (not first and step >= STEPS - 2):
            lower = lower + jnp.where(steps[entry + 4] == 1, LOW, 0.0)
        score = jnp.concatenate([upper, lower], axis=0)
        new = jnp.max(score, axis=0, keepdims=True)
        if not fresh:
            source = carried if not first and step == 0 else None
            old = best[part, :, at] if source is None else packed_in[0, part, :, at]
            new = jnp.maximum(old, new)
        best[part, :, at] = new
        weight = jnp.exp2((score - new) * scale).astype(jnp.bfloat16)
        if unit + AHEAD < units:
            scores.append(raw(unit + AHEAD))
        more = jnp.dot(turned, weight, preferred_element_type=jnp.float32)[: HEAD + 8]
        if not fresh:
            before = sums[part, :, at] if source is None else carried[0, part, :, at]
            more = before * jnp.exp2((old - new) * scale) + more
        sums[part, :, at] = more

    if not last:
        return
    for part in range(2):
        share = 1.0 / sums[part, HEAD : HEAD + 1, :]
        for group in range(0, GROUPS, 2):
            at = slice(group * half, (group + 2) * half)
            done = (sums[part, :HEAD, at] * share[:, at]).T.astype(out.dtype)
            for side in range(2):
                out[
                    part * half : (part + 1) * half, (group + side) * HEAD : (group + side + 1) * HEAD
                ] = done[side * half : (side + 1) * half]


def attend(queries, arrays, moves, steps, carried=None, last=True):
    tokens, width = queries.shape
    half = tokens // 2
    stack = GROUPS * half
    segments = 1 + max(piece[1] for pieces in moves for piece in pieces)
    first = carried is None

    def body(*refs):
        attend_kernel(moves, first, last, *refs)

    state_specs = [
        pl.BlockSpec((1, 2, HEAD + 8, stack), lambda h, s: (h, 0, 0, 0)),
        pl.BlockSpec((1, 2, 1, stack), lambda h, s: (h, 0, 0, 0)),
    ]
    wide = pl.BlockSpec((tokens, GROUPS * HEAD), lambda h, s: (0, h))
    if last:
        out_shape = jax.ShapeDtypeStruct((tokens, width), jnp.bfloat16)
        out_specs = wide
    else:
        out_shape = [
            pltpu.HBM((KV_HEADS, 2, HEAD + 8, stack), jnp.float32),
            pltpu.HBM((KV_HEADS, 2, 1, stack), jnp.float32),
        ]
        out_specs = state_specs
    if not first:
        carried = [pltpu.with_memory_space_constraint(a, pltpu.HBM) for a in carried]
    queries = pltpu.with_memory_space_constraint(queries, pltpu.HBM)
    return pl.pallas_call(
        body,
        out_shape=out_shape,
        grid_spec=pltpu.PrefetchScalarGridSpec(
            num_scalar_prefetch=1,
            grid=(KV_HEADS,),
            in_specs=[wide]
            + [pl.BlockSpec(memory_space=pltpu.VMEM)] * len(arrays)
            + ([] if first else state_specs),
            out_specs=out_specs,
            scratch_shapes=[
                pltpu.VMEM((segments, half, HEAD), jnp.bfloat16),
                pltpu.VMEM((segments, half, HEAD), jnp.bfloat16),
                pltpu.VMEM((half, stack), jnp.float32),
            ]
            + (
                [
                    pltpu.VMEM((2, 1, stack), jnp.float32),
                    pltpu.VMEM((2, HEAD + 8, stack), jnp.float32),
                ]
                if last
                else []
            ),
        ),
        compiler_params=pltpu.CompilerParams(vmem_limit_bytes=40 << 20, flags=FLAGS),
        cost_estimate=pl.CostEstimate(
            flops=2 * 2 * Q_HEADS * (segments + 1) * half * half * HEAD * 2,
            transcendentals=Q_HEADS * (segments + 1) * half * half,
            bytes_accessed=30 << 20,
        ),
        name="attend_last" if last else "attend_first",
    )(steps, queries, *arrays, *(() if first else carried))


SPAN = 256
STEPS = 5
AHEAD = 12
FLAGS = {}


def shards(
    hidden, queries, weights_old, gradient_old, first_old, second_old, old_owner, new_owner, offsets
):
    devices = old_owner.shape[0]
    row_count, proj_width = weights_old.shape
    tok_rows = hidden.shape[1]
    half_tok = tok_rows // 2
    sizes = [lax.axis_size(a) for a in ALL]
    copies = adam_step(weights_old, gradient_old, first_old, second_old)[0].astype(jnp.bfloat16)
    gathered = lax.all_gather(copies, TORUS, axis=0, tiled=False).reshape(
        devices, row_count, proj_width
    )
    owner_at = old_owner.reshape(sizes).transpose([ALL.index(a) for a in TORUS]).reshape(devices)
    source = invert(owner_at)
    states = lax.optimization_barrier((weights_old, gradient_old, first_old, second_old, copies))[:4]
    moved = relocate(jnp.stack(adam_step(*states)), new_owner, old_owner)

    x_at, zl_at = lax.axis_index("x"), lax.axis_index("zl")
    pair = lax.axis_size("zl")
    table = offsets[0]
    mine = table[x_at * pair + zl_at]
    local = jnp.arange(tok_rows, dtype=jnp.int32)
    query_pos = jnp.where(local < half_tok, mine[0] + local, mine[1] + local - half_tok)
    exponent = jnp.arange(HEAD // 2, dtype=jnp.float32) * (2.0 / HEAD)
    inv_freq = jnp.power(rope_base, -exponent)
    angles = query_pos.astype(jnp.float32)[:, None] * inv_freq
    cosine, sine = jnp.cos(angles), jnp.sin(angles)
    cosine = jnp.concatenate([cosine, cosine], axis=1)
    sine = jnp.concatenate([-sine, sine], axis=1)

    xs = lax.axis_size("x")
    steps = plan(table.reshape(-1), jnp.stack([x_at, zl_at]).astype(jnp.int32))

    gathered, source, cosine, sine, steps, moved = lax.optimization_barrier(
        (gathered, source, cosine, sine, steps, moved)
    )
    weights_new, first_new, second_new = (moved[0], moved[1], moved[2])
    in_hbm = pltpu.with_memory_space_constraint(hidden[0], pltpu.HBM)
    rows_own = project(in_hbm, gathered, source, cosine, sine)
    near = [(i, i ^ 1) for i in range(pair)]
    ahead = [(i, (i + 1) % xs) for i in range(xs)]
    behind = [(i, (i - 1) % xs) for i in range(xs)]
    z_rows = lax.ppermute(rows_own, "zl", near)
    left = lax.ppermute(rows_own, "x", ahead)
    right = lax.ppermute(rows_own, "x", behind)
    left_z = lax.ppermute(left, "zl", near)
    right_z = lax.ppermute(z_rows, "x", behind)
    far = lax.ppermute(left, "x", ahead)
    halves = [(0, 0, half_tok), (half_tok, 1, half_tok)]
    moves = [[(start, 2 * i + seg, 0, size) for start, seg, size in halves] for i in range(4)]
    state = attend(queries[0], [rows_own, z_rows, left, right], moves, steps, last=False)
    left_z, right_z, far, state = lax.optimization_barrier((left_z, right_z, far, state))
    first_rows = half_tok - tok_rows // 12
    cut = (first_rows + tok_rows) // 2
    last_z = lax.ppermute(far[:first_rows], "zl", near)
    last_left = lax.ppermute(left_z[first_rows:cut], "x", ahead)
    last_right = lax.ppermute(right_z[cut:], "x", behind)
    moves = moves[:3] + [
        [(0, 6, 0, first_rows)],
        [(0, 6, first_rows, half_tok - first_rows), (half_tok - first_rows, 7, 0, cut - half_tok)],
        [(0, 7, cut - half_tok, tok_rows - cut)],
    ]
    attended = attend(
        queries[0], [left_z, right_z, far, last_z, last_left, last_right], moves, steps, carried=state
    )
    return (weights_new, first_new, second_new, attended[None])


def solution(mesh):
    grid = Mesh(mesh.devices.reshape(2, 4, 2, 4, 2), ALL)
    in_specs = (
        P(DP, CTX, None),
        P(DP, CTX, None),
        P(ALL, None),
        P(ALL, None),
        P(ALL, None),
        P(ALL, None),
        P(),
        P(),
        P(DP, None, None),
    )
    out_specs = (
        P(ALL, None),
        P(ALL, None),
        P(ALL, None),
        P(DP, CTX, None),
    )
    return jax.shard_map(shards, mesh=grid, in_specs=in_specs, out_specs=out_specs, check_vma=False)
```

```python
import math

import jax
import jax.numpy as jnp
from jax import lax
from jax.experimental import pallas as pl
from jax.experimental.pallas import tpu as pltpu
from jax.sharding import Mesh
from jax.sharding import PartitionSpec as P

HEAD = 128
KV_HEADS = 4
Q_HEADS = 32
GROUPS = Q_HEADS // KV_HEADS
DP = ("zh", "y", "c")
CTX = ("x", "zl")
ALL = DP + CTX
TORUS = ("zh", "zl", "x", "y", "c")
LOW = -1e30


learn_rate = 0.0003
beta_one = 0.9
beta_two = 0.95
adam_eps = 1e-08
decay_rate = 0.1
step_number = 1000
corr_one = 1.0 - beta_one**step_number
corr_two = 1.0 - beta_two**step_number
rope_base = 500000.0


def in_blocks(value, dim, peers):
    before, after = (value.shape[:dim], value.shape[dim + 1 :])
    return jnp.moveaxis(value.reshape(*before, peers, -1, *after), dim, 0)


def adam_step(weights, gradient, first_mom, second_mom):
    first_next = beta_one * first_mom + (1.0 - beta_one) * gradient
    second_next = beta_two * second_mom + (1.0 - beta_two) * gradient * gradient
    direction = first_next / corr_one / (jnp.sqrt(second_next / corr_two) + adam_eps)
    weights_next = weights - learn_rate * (direction + decay_rate * weights)
    return (weights_next, first_next, second_next)


def invert(owners):
    devices = owners.shape[0]
    return jnp.zeros((devices,), jnp.int32).at[owners].set(jnp.arange(devices, dtype=jnp.int32))


def relocate(stacked, new_owner, old_owner):
    states_count, row_count, proj_width = stacked.shape
    devices = new_owner.shape[0]
    col_count = proj_width // devices
    outgoing = stacked.reshape(states_count, row_count, devices, col_count).transpose(2, 0, 3, 1)
    outgoing = jnp.take(outgoing, new_owner, axis=0)
    incoming = lax.all_to_all(outgoing, ALL, split_axis=0, concat_axis=0, tiled=True)
    ordered = jnp.take(incoming, invert(old_owner), axis=0)
    return ordered.transpose(1, 2, 0, 3).reshape(states_count, col_count, devices * row_count)


def project_kernel(source, hidden, gathered, cosine, sine, out, rows, cols, sums, row_sem, col_sem):
    blocks, block_rows, _ = gathered.shape
    tokens, width = hidden.shape
    chunks = row_sem.shape[0]
    per = blocks // chunks
    span = width // chunks

    def row_copy(block, chunk):
        return pltpu.make_async_copy(
            gathered.at[source[block]],
            rows.at[pl.ds(pl.multiple_of(block * block_rows, block_rows), block_rows)],
            row_sem.at[chunk],
        )

    def col_copy(chunk):
        return pltpu.make_async_copy(
            hidden.at[:, pl.ds(chunk * span, span)],
            cols.at[:, pl.ds(chunk * span, span)],
            col_sem.at[chunk],
        )

    for chunk in range(chunks):
        col_copy(chunk).start()

        def issue(i, carry, chunk=chunk):
            row_copy(chunk * per + i, chunk).start()
            return carry

        lax.fori_loop(0, per, issue, 0)
    for chunk in range(chunks):
        col_copy(chunk).wait()
        whole = rows.at[pl.ds(chunk * span, span)]
        pltpu.make_async_copy(whole, whole, row_sem.at[chunk]).wait()
        part = jnp.dot(
            cols[:, chunk * span : (chunk + 1) * span],
            rows[chunk * span : (chunk + 1) * span, :],
            preferred_element_type=jnp.float32,
        )
        if chunk == 0:
            sums[...] = part
        else:
            sums[...] += part
    for head in range(KV_HEADS):
        key = sums[:, head * HEAD : (head + 1) * HEAD]
        turned = pltpu.roll(key, HEAD // 2, 1)
        out[:, head * HEAD : (head + 1) * HEAD] = (
            key * cosine[...] + turned * sine[...]
        ).astype(out.dtype)
    key_width = KV_HEADS * HEAD
    out[:, key_width:] = sums[:, key_width:].astype(out.dtype)


def project(hidden, gathered, source, cosine, sine):
    tokens, width = hidden.shape
    blocks, block_rows, features = gathered.shape
    chunks = 16
    return pl.pallas_call(
        project_kernel,
        out_shape=jax.ShapeDtypeStruct((tokens, features), jnp.bfloat16),
        grid_spec=pltpu.PrefetchScalarGridSpec(
            num_scalar_prefetch=1,
            grid=(1,),
            in_specs=[
                pl.BlockSpec(memory_space=pltpu.HBM),
                pl.BlockSpec(memory_space=pltpu.HBM),
                pl.BlockSpec((tokens, HEAD), lambda i, s: (0, 0)),
                pl.BlockSpec((tokens, HEAD), lambda i, s: (0, 0)),
            ],
            out_specs=pl.BlockSpec((tokens, features), lambda i, s: (0, 0)),
            scratch_shapes=[
                pltpu.VMEM((width, features), jnp.bfloat16),
                pltpu.VMEM((tokens, width), jnp.bfloat16),
                pltpu.VMEM((tokens, features), jnp.float32),
                pltpu.SemaphoreType.DMA((chunks,)),
                pltpu.SemaphoreType.DMA((chunks,)),
            ],
        ),
        compiler_params=pltpu.CompilerParams(vmem_limit_bytes=44 << 20),
        name="project",
    )(source, hidden, gathered, cosine, sine)


ENTRY = 5
ARRIVALS = ((0, 0), (0, 1), (-1, 0), (1, 0), (-1, 1), (1, 1), (2, 0), (2, 1))


def plan_kernel(xs, zs, table, place, out, lows, highs):
    x_at, z_at = place[0], place[1]
    mine = table[2 * (x_at * zs + z_at)]
    for call in range(2):
        skip = 1 - call
        shards_in = ARRIVALS[4 * call : 4 * call + 4]
        others = 4 - skip
        low_count = jnp.int32(0)
        high_count = jnp.int32(others if skip else 0)
        for slot in range(skip, 4):
            dx, dz = shards_in[slot]
            low = table[2 * ((x_at + dx + xs) % xs * zs + (z_at + dz) % zs)]
            under = jnp.where(low < mine, 1, 0)
            if skip:
                highs[slot - skip] = 2 * slot
            lows[low_count] = 2 * slot
            highs[high_count] = 2 * slot + 1
            low_count = low_count + under
            high_count = high_count + 1 - under
        begin = call * STEPS * ENTRY
        shift = 0
        if skip:
            fixed = (0, 0, lows[0], 0, jnp.where(low_count == 0, 1, 0), 1, 1, 0, 0, 0)
            for i, value in enumerate(fixed):
                out[begin + i] = jnp.int32(value)
            shift = 1
            low_count = jnp.maximum(low_count - 1, 0)
        low_full, high_full = low_count // 2, high_count // 2
        low_odd, high_odd = low_count % 2, high_count % 2
        for step in range(STEPS - 2):
            after = step - low_full - high_full
            in_low = step < low_full
            full = after < 0
            end_low = (after == 0) & (low_odd == 1)
            end_high = (after == low_odd) & (high_odd == 1)
            is_low = in_low | end_low
            at_low = jnp.where(in_low, 2 * step, jnp.maximum(low_count - 1, 0))
            at_high = jnp.where(full, jnp.maximum(2 * (step - low_full), 0), jnp.maximum(high_count - 1, 0))
            key_a = jnp.where(is_low, lows[shift + at_low], highs[at_high])
            key_a = jnp.where(full | end_low | end_high, key_a, 0)
            key_b = jnp.where(is_low, lows[shift + at_low + 1], highs[at_high + 1])
            key_b = jnp.where(full, key_b, key_a)
            entry = begin + (2 + step) * ENTRY
            out[entry] = jnp.where(is_low, 0, 1)
            out[entry + 1] = key_a
            out[entry + 2] = key_b
            out[entry + 3] = jnp.where(full | end_low | end_high, 0, 1)
            out[entry + 4] = jnp.where(full, 0, 1)


def plan(table, place):
    xs, zs = lax.axis_size("x"), lax.axis_size("zl")

    def body(*refs):
        plan_kernel(xs, zs, *refs)

    in_smem = pl.BlockSpec(memory_space=pltpu.SMEM)
    return pl.pallas_call(
        body,
        out_shape=jax.ShapeDtypeStruct((2 * STEPS * ENTRY,), jnp.int32),
        in_specs=[in_smem, in_smem],
        out_specs=in_smem,
        scratch_shapes=[pltpu.SMEM((16,), jnp.int32), pltpu.SMEM((16,), jnp.int32)],
        name="plan",
    )(table, place)


def attend_kernel(moves, first, last, steps, queries, *refs):
    sources = len(moves)
    pairs = refs[:sources]
    rest = list(refs[sources:])
    if not first:
        carried, packed_in = rest.pop(0), rest.pop(0)
    if last:
        out = rest.pop(0)
    else:
        kept, packed_out = rest.pop(0), rest.pop(0)
    if last:
        key_rows, value_rows, corner, best, sums = rest
    else:
        key_rows, value_rows, corner = rest
        best, sums = packed_out.at[0], kept.at[0]
    half = queries.shape[0] // 2
    stack = GROUPS * half
    scale = math.log2(math.e) / math.sqrt(HEAD)
    span = SPAN
    chunks = stack // span

    if first:

        @pl.when(pl.program_id(0) == 0)
        def _():
            lane = lax.broadcasted_iota(jnp.int32, corner.shape, 1)
            row = lax.broadcasted_iota(jnp.int32, corner.shape, 0)
            corner[...] = jnp.where(row <= lax.rem(lane, half), 0.0, LOW)

    key_at = pl.multiple_of(pl.program_id(0) * HEAD, HEAD)
    value_at = pl.multiple_of((KV_HEADS + pl.program_id(0)) * HEAD, HEAD)
    for source, pieces in enumerate(moves):
        for start, segment, place, size in pieces:
            rows = slice(start, start + size)
            key_rows[segment, place : place + size] = pairs[source][rows, pl.ds(key_at, HEAD)]
            value_rows[segment, place : place + size] = pairs[source][rows, pl.ds(value_at, HEAD)]
    if not first:
        best[0] = packed_in[0, 0]
        sums[0] = carried[0, 0]

    seen = []
    for step in range(STEPS):
        entry = (step if first else STEPS + step) * ENTRY
        fresh = first and step < 2
        if not first and step < 2:
            part, key_a, key_b = 1, 4 * step, 4 * step + 2
        else:
            part = step if fresh else steps[entry]
            key_a, key_b = steps[entry + 1], steps[entry + 2]
        key = jnp.concatenate([key_rows[key_a], key_rows[key_b]], axis=0)
        value = jnp.concatenate([value_rows[key_a], value_rows[key_b]], axis=0)
        turned = jnp.concatenate([value.T, jnp.ones((16, 2 * half), value.dtype)], axis=0)
        seen.append((entry, fresh, part, key, turned))

    def raw(unit):
        _, _, part, key, _ = seen[unit // chunks]
        at = unit % chunks * span
        pieces = []
        while at < unit % chunks * span + span:
            group, row = at // half, at % half
            size = min(half - row, unit % chunks * span + span - at)
            rows = pl.ds(part * half + row, size)
            if not isinstance(part, int):
                rows = pl.ds(pl.multiple_of(part * half, half) + row, size)
            pieces.append(queries[rows, group * HEAD : (group + 1) * HEAD])
            at += size
        return lax.dot_general(
            key, jnp.concatenate(pieces, axis=0), (((1,), (1,)), ((), ())), preferred_element_type=jnp.float32
        )

    units = STEPS * chunks
    scores = [raw(unit) for unit in range(AHEAD)]
    for unit in range(units):
        step = unit // chunks
        entry, fresh, part, key, turned = seen[step]
        at = slice(unit % chunks * span, (unit % chunks + 1) * span)
        score = scores[unit]
        scores[unit] = None
        upper, lower = score[:half], score[half:]
        if fresh:
            upper = upper + corner[:, at]
        if not first and step == STEPS - 1:
            upper = upper + jnp.where(steps[entry + 3] == 1, LOW, 0.0)
        if (first and step in (0, STEPS - 1)) or (not first and step >= STEPS - 2):
            lower = lower + jnp.where(steps[entry + 4] == 1, LOW, 0.0)
        score = jnp.concatenate([upper, lower], axis=0)
        new = jnp.max(score, axis=0, keepdims=True)
        if not fresh:
            source = carried if not first and step == 0 else None
            old = best[part, :, at] if source is None else packed_in[0, part, :, at]
            new = jnp.maximum(old, new)
        best[part, :, at] = new
        weight = jnp.exp2((score - new) * scale).astype(jnp.bfloat16)
        if unit + AHEAD < units:
            scores.append(raw(unit + AHEAD))
        more = jnp.dot(turned, weight, preferred_element_type=jnp.float32)[: HEAD + 8]
        if not fresh:
            before = sums[part, :, at] if source is None else carried[0, part, :, at]
            more = before * jnp.exp2((old - new) * scale) + more
        sums[part, :, at] = more

    if not last:
        return
    for part in range(2):
        share = 1.0 / sums[part, HEAD : HEAD + 1, :]
        for group in range(0, GROUPS, 2):
            at = slice(group * half, (group + 2) * half)
            done = (sums[part, :HEAD, at] * share[:, at]).T.astype(out.dtype)
            for side in range(2):
                out[
                    part * half : (part + 1) * half, (group + side) * HEAD : (group + side + 1) * HEAD
                ] = done[side * half : (side + 1) * half]


def attend(queries, arrays, moves, steps, carried=None, last=True):
    tokens, width = queries.shape
    half = tokens // 2
    stack = GROUPS * half
    segments = 1 + max(piece[1] for pieces in moves for piece in pieces)
    first = carried is None

    def body(*refs):
        attend_kernel(moves, first, last, *refs)

    state_specs = [
        pl.BlockSpec((1, 2, HEAD + 8, stack), lambda h, s: (h, 0, 0, 0)),
        pl.BlockSpec((1, 2, 1, stack), lambda h, s: (h, 0, 0, 0)),
    ]
    wide = pl.BlockSpec((tokens, GROUPS * HEAD), lambda h, s: (0, h))
    if last:
        out_shape = jax.ShapeDtypeStruct((tokens, width), jnp.bfloat16)
        out_specs = wide
    else:
        out_shape = [
            pltpu.HBM((KV_HEADS, 2, HEAD + 8, stack), jnp.float32),
            pltpu.HBM((KV_HEADS, 2, 1, stack), jnp.float32),
        ]
        out_specs = state_specs
    if not first:
        carried = [pltpu.with_memory_space_constraint(a, pltpu.HBM) for a in carried]
    queries = pltpu.with_memory_space_constraint(queries, pltpu.HBM)
    return pl.pallas_call(
        body,
        out_shape=out_shape,
        grid_spec=pltpu.PrefetchScalarGridSpec(
            num_scalar_prefetch=1,
            grid=(KV_HEADS,),
            in_specs=[wide]
            + [pl.BlockSpec(memory_space=pltpu.VMEM)] * len(arrays)
            + ([] if first else state_specs),
            out_specs=out_specs,
            scratch_shapes=[
                pltpu.VMEM((segments, half, HEAD), jnp.bfloat16),
                pltpu.VMEM((segments, half, HEAD), jnp.bfloat16),
                pltpu.VMEM((half, stack), jnp.float32),
            ]
            + (
                [
                    pltpu.VMEM((2, 1, stack), jnp.float32),
                    pltpu.VMEM((2, HEAD + 8, stack), jnp.float32),
                ]
                if last
                else []
            ),
        ),
        compiler_params=pltpu.CompilerParams(vmem_limit_bytes=40 << 20, flags=FLAGS),
        cost_estimate=pl.CostEstimate(
            flops=2 * 2 * Q_HEADS * (segments + 1) * half * half * HEAD * 2,
            transcendentals=Q_HEADS * (segments + 1) * half * half,
            bytes_accessed=30 << 20,
        ),
        name="attend_last" if last else "attend_first",
    )(steps, queries, *arrays, *(() if first else carried))


SPAN = 256
STEPS = 5
AHEAD = 12
FLAGS = {}


def shards(
    hidden, queries, weights_old, gradient_old, first_old, second_old, old_owner, new_owner, offsets
):
    devices = old_owner.shape[0]
    row_count, proj_width = weights_old.shape
    tok_rows = hidden.shape[1]
    half_tok = tok_rows // 2
    sizes = [lax.axis_size(a) for a in ALL]
    copies = adam_step(weights_old, gradient_old, first_old, second_old)[0].astype(jnp.bfloat16)
    gathered = lax.all_gather(copies, TORUS, axis=0, tiled=False).reshape(
        devices, row_count, proj_width
    )
    owner_at = old_owner.reshape(sizes).transpose([ALL.index(a) for a in TORUS]).reshape(devices)
    source = invert(owner_at)
    states = lax.optimization_barrier((weights_old, gradient_old, first_old, second_old, copies))[:4]
    moved = relocate(jnp.stack(adam_step(*states)), new_owner, old_owner)

    x_at, zl_at = lax.axis_index("x"), lax.axis_index("zl")
    pair = lax.axis_size("zl")
    table = offsets[0]
    mine = table[x_at * pair + zl_at]
    local = jnp.arange(tok_rows, dtype=jnp.int32)
    query_pos = jnp.where(local < half_tok, mine[0] + local, mine[1] + local - half_tok)
    exponent = jnp.arange(HEAD // 2, dtype=jnp.float32) * (2.0 / HEAD)
    inv_freq = jnp.power(rope_base, -exponent)
    angles = query_pos.astype(jnp.float32)[:, None] * inv_freq
    cosine, sine = jnp.cos(angles), jnp.sin(angles)
    cosine = jnp.concatenate([cosine, cosine], axis=1)
    sine = jnp.concatenate([-sine, sine], axis=1)

    xs = lax.axis_size("x")
    steps = plan(table.reshape(-1), jnp.stack([x_at, zl_at]).astype(jnp.int32))

    gathered, source, cosine, sine, steps, moved = lax.optimization_barrier(
        (gathered, source, cosine, sine, steps, moved)
    )
    weights_new, first_new, second_new = (moved[0], moved[1], moved[2])
    in_hbm = pltpu.with_memory_space_constraint(hidden[0], pltpu.HBM)
    rows_own = project(in_hbm, gathered, source, cosine, sine)
    near = [(i, i ^ 1) for i in range(pair)]
    ahead = [(i, (i + 1) % xs) for i in range(xs)]
    behind = [(i, (i - 1) % xs) for i in range(xs)]
    z_rows = lax.ppermute(rows_own, "zl", near)
    left = lax.ppermute(rows_own, "x", ahead)
    right = lax.ppermute(rows_own, "x", behind)
    left_z = lax.ppermute(left, "zl", near)
    right_z = lax.ppermute(z_rows, "x", behind)
    far = lax.ppermute(left, "x", ahead)
    halves = [(0, 0, half_tok), (half_tok, 1, half_tok)]
    moves = [[(start, 2 * i + seg, 0, size) for start, seg, size in halves] for i in range(4)]
    state = attend(queries[0], [rows_own, z_rows, left, right], moves, steps, last=False)
    left_z, right_z, far, state = lax.optimization_barrier((left_z, right_z, far, state))
    first_rows = half_tok - tok_rows // 12
    cut = (first_rows + tok_rows) // 2
    last_z = lax.ppermute(far[:first_rows], "zl", near)
    last_left = lax.ppermute(left_z[first_rows:cut], "x", ahead)
    last_right = lax.ppermute(right_z[cut:], "x", behind)
    moves = moves[:3] + [
        [(0, 6, 0, first_rows)],
        [(0, 6, first_rows, half_tok - first_rows), (half_tok - first_rows, 7, 0, cut - half_tok)],
        [(0, 7, cut - half_tok, tok_rows - cut)],
    ]
    attended = attend(
        queries[0], [left_z, right_z, far, last_z, last_left, last_right], moves, steps, carried=state
    )
    return (weights_new, first_new, second_new, attended[None])


def solution(mesh):
    grid = Mesh(mesh.devices.reshape(2, 4, 2, 4, 2), ALL)
    in_specs = (
        P(DP, CTX, None),
        P(DP, CTX, None),
        P(ALL, None),
        P(ALL, None),
        P(ALL, None),
        P(ALL, None),
        P(),
        P(),
        P(DP, None, None),
    )
    out_specs = (
        P(ALL, None),
        P(ALL, None),
        P(ALL, None),
        P(DP, CTX, None),
    )
    return jax.shard_map(shards, mesh=grid, in_specs=in_specs, out_specs=out_specs, check_vma=False)
```
